512 devices in a mesh: ctx: 16 (over x, z_hi, core), ch: 32 (over z_lo, y).
Axes of the slice: x: 4, y: 4, z: 16 (z_hi: 2, z_lo: 8; z = z_hi * 8 + z_lo), core: 2. Of those that a mesh axis runs over, the one named last changes fastest.
Arguments:
- query_gate: bfloat16 [4096, 8192], P(('ctx', 'ch')), may hold values from -6 to 6
- key_gate: bfloat16 [4096, 8192], P(('ctx', 'ch')), may hold values from -6 to 6
- value_proj: bfloat16 [4096, 8192], P(('ctx', 'ch')), may hold values from -6 to 6
- grad_out: bfloat16 [4096, 8192], P(('ctx', 'ch')), may hold values from -0.375 to 0.375
- long_filters: float32 [512, 4096], P('ch', 'ctx'), may hold values from -0.09375 to 0.09375
Outputs:
- grad_query: bfloat16 [4096, 8192], P(('ctx', 'ch'))
- grad_key: bfloat16 [4096, 8192], P(('ctx', 'ch'))
- grad_value: bfloat16 [4096, 8192], P(('ctx', 'ch'))
- grad_filters: float32 [512, 4096], P('ch', 'ctx')
The draws below stay inside these ranges and needn't reach their ends.
All inputs are finite; a program needn't handle non-finite values.
Results may differ from the reference program's by a relative error of at most 0.0058.
Values may be sent and summed in bfloat16 or wider, within the bound.
No kernel may reach another device: no remote copies, remote signals or barrier semaphores. Data moves between devices by JAX's collectives and lax.ppermute only.
A program may use at most 64 MiB of HBM per device.

```python
import jax
import jax.numpy as jnp
from jax import lax

D = 8192
GROUP_CH = 16
GROUPS = 512
SEQ = 4096


def block_levels(rng, shape, pieces, low, high):
    def one(dim, blocks):
        draws = jax.random.uniform(jax.random.fold_in(jax.random.fold_in(rng, 6), dim), (blocks,), jnp.float32, low / len(pieces), high / len(pieces))
        return jnp.repeat(jnp.exp(draws), shape[dim] // blocks).reshape((-1,) + (1,) * (len(shape) - dim - 1))

    gain = one(*pieces[0])
    for cut in pieces[1:]:
        gain = gain * one(*cut)
    return gain


def scatter_about(key, extent, scale, most, shards=(), kind=jnp.bfloat16):
    level = block_levels(key, extent, shards, -0.22, 0.18) if shards else 1.0
    entries = jax.random.normal(key, extent, jnp.float32) * scale * level
    return jnp.minimum(jnp.maximum(entries, -most), most).astype(kind)


def setup_inputs(seed: int = 0) -> dict:
    arg_keys = jax.random.split(jax.random.key(seed), 6)
    return {
        "query_gate": scatter_about(arg_keys[0], (SEQ, D), 1.0, 6.0, ((0, 512),)),
        "key_gate": scatter_about(arg_keys[1], (SEQ, D), 1.0, 6.0, ((0, 512),)),
        "value_proj": scatter_about(arg_keys[2], (SEQ, D), 1.0, 6.0, ((0, 512),)),
        "grad_out": scatter_about(arg_keys[3], (SEQ, D), 0.0625, 0.375, ((0, 512),)),
        "long_filters": scatter_about(arg_keys[4], (GROUPS, SEQ), SEQ ** -0.5, 0.09375, ((0, 32), (1, 16)), jnp.float32),
    }


def reference(query_gate, key_gate, value_proj, grad_out, long_filters):
    seq_len = query_gate.shape[0]
    width = query_gate.shape[1]
    signal = (key_gate.astype(jnp.float32) * value_proj.astype(jnp.float32)).astype(jnp.bfloat16)
    upstream = (grad_out.astype(jnp.float32) * query_gate.astype(jnp.float32)).astype(jnp.bfloat16)
    block_width = 256
    group_count = block_width // GROUP_CH
    length = 2 * seq_len

    def per_block(index):
        start = index * block_width
        sig_vals = lax.dynamic_slice_in_dim(signal, start, block_width, 1).astype(jnp.float32)
        up_vals = lax.dynamic_slice_in_dim(upstream, start, block_width, 1).astype(jnp.float32)
        group_taps = lax.dynamic_slice_in_dim(long_filters, index * group_count, group_count, 0)
        taps = jnp.repeat(group_taps, GROUP_CH, axis=0).T
        sig_freq = jnp.fft.rfft(sig_vals, n=length, axis=0)
        up_freq = jnp.fft.rfft(up_vals, n=length, axis=0)
        tap_freq = jnp.fft.rfft(taps, n=length, axis=0)
        convolved = jnp.fft.irfft(tap_freq * sig_freq, n=length, axis=0)[:seq_len]
        correlated = jnp.fft.irfft(jnp.conj(tap_freq) * up_freq, n=length, axis=0)[:seq_len]
        lagged = jnp.fft.irfft(up_freq * jnp.conj(sig_freq), n=length, axis=0)[:seq_len]
        grouped = lagged.reshape(seq_len, group_count, GROUP_CH).sum(axis=2)
        return convolved, correlated, grouped

    block_ids = jnp.arange(width // block_width, dtype=jnp.int32)
    convolved, correlated, grouped = lax.map(per_block, block_ids)
    convolved = convolved.transpose(1, 0, 2).reshape(seq_len, width)
    correlated = correlated.transpose(1, 0, 2).reshape(seq_len, width)
    convolved = lax.optimization_barrier(convolved.astype(jnp.bfloat16)).astype(jnp.float32)
    correlated = lax.optimization_barrier(correlated.astype(jnp.bfloat16)).astype(jnp.float32)
    grad_filters = grouped.transpose(0, 2, 1).reshape(width // GROUP_CH, seq_len)
    grad_query = (grad_out.astype(jnp.float32) * convolved).astype(jnp.bfloat16)
    grad_key = (correlated * value_proj.astype(jnp.float32)).astype(jnp.bfloat16)
    grad_value = (correlated * key_gate.astype(jnp.float32)).astype(jnp.bfloat16)
    return grad_query, grad_key, grad_value, grad_filters
```

```python
import jax
import jax.numpy as jnp
from jax import lax
from jax.experimental import pallas as pl
from jax.experimental.pallas import tpu as pltpu
from jax.sharding import PartitionSpec as P

CH = 16
TOK = 8
ROWS = 128
F32 = jnp.float32
BF16 = jnp.bfloat16


def lane_of(shape):
    return lax.broadcasted_iota(jnp.int32, shape, 1)


def row_of(shape):
    return lax.broadcasted_iota(jnp.int32, shape, 0)


def swap_segments(x):
    row, seg = row_of(x.shape), lane_of(x.shape) // CH
    for bit in range(3):
        step = 1 << bit
        row_bit, seg_bit = (row >> bit) & 1, (seg >> bit) & 1
        down = pltpu.roll(pltpu.roll(x, step, 0), 128 - CH * step, 1)
        up = pltpu.roll(pltpu.roll(x, TOK - step, 0), CH * step, 1)
        x = jnp.where(row_bit == seg_bit, x, jnp.where(row_bit == 1, down, up))
    return x


def pack_kernel(q_ref, k_ref, v_ref, g_ref, o_ref, wide):
    for block in range(q_ref.shape[1] // 128):
        j, half = divmod(block, 2)
        lanes = pl.ds(block * 128, 128)
        for a, (x_ref, y_ref) in enumerate(((k_ref, v_ref), (g_ref, q_ref))):
            prod = (x_ref[:, lanes].astype(F32) * y_ref[:, lanes].astype(F32)).astype(BF16)
            wide[pl.ds(8 * half * 64 + 2 * j + a, 8, stride=64), :] = swap_segments(prod.astype(F32))
    o_ref[...] = wide[...].astype(BF16)


def unpack_kernel(r_ref, k_ref, v_ref, g_ref, gq_ref, gk_ref, gv_ref, wide):
    wide[...] = r_ref[...].astype(F32)
    for block in range(k_ref.shape[1] // 128):
        j, half = divmod(block, 2)
        lanes = pl.ds(block * 128, 128)
        conv = swap_segments(wide[pl.ds(8 * half * 64 + 2 * j, 8, stride=64), :])
        corr = swap_segments(wide[pl.ds(8 * half * 64 + 2 * j + 1, 8, stride=64), :])
        gq_ref[:, lanes] = (g_ref[:, lanes].astype(F32) * conv).astype(BF16)
        gk_ref[:, lanes] = (corr * v_ref[:, lanes].astype(F32)).astype(BF16)
        gv_ref[:, lanes] = (corr * k_ref[:, lanes].astype(F32)).astype(BF16)


def toeplitz_kernel(h_ref, hi_ref, lo_ref, t_ref, base):
    width = h_ref.shape[1]
    lane8, row8 = lane_of((8, width)), row_of((8, width))
    for p in range(TOK):
        skew = jnp.broadcast_to(h_ref[pl.ds(p, 1), :], (8, width))
        for bit in range(3):
            skew = jnp.where((row8 >> bit) & 1 == 1, pltpu.roll(skew, 1 << bit, 1), skew)
        for r in range(ROWS // 8):
            part = pltpu.roll(skew, 8 * r, 1) if r else skew
            base[pl.ds(8 * r, 8), :] = jnp.where(lane8 >= row8 + 8 * r, part, 0.0)
        whole = base[...]
        high = whole.astype(BF16)
        hi_ref[pl.ds(p * ROWS, ROWS), :] = high
        lo_ref[pl.ds(p * ROWS, ROWS), :] = (whole - high.astype(F32)).astype(BF16)
        for m in range(width // 128):
            flip = whole[:, m * 128 : (m + 1) * 128].T
            high = flip.astype(BF16)
            at = pl.ds(p * width + m * 128, 128)
            t_ref[at, pl.ds(0, 128)] = high
            t_ref[at, pl.ds(128, 128)] = (flip - high.astype(F32)).astype(BF16)


def group_kernel(r_ref, hi_ref, lo_ref, t_ref, o_ref, g_ref, wide, lhs, ahead):
    count = r_ref.shape[0] // 2
    nblk = count // ROWS
    wide[...] = r_ref[...].astype(F32)
    sig = wide[pl.ds(0, count, stride=2), :]
    ups = wide[pl.ds(1, count, stride=2), :]
    sig_t = jnp.concatenate([sig[b * 128 : b * 128 + 128].T for b in range(nblk)], axis=1)
    ups_t = jnp.concatenate([ups[b * 128 : b * 128 + 128].T for b in range(nblk)], axis=1)
    lane = lane_of(sig_t.shape)
    sig_prev = jnp.where(lane == 0, 0.0, pltpu.roll(sig_t, 1, 1)).astype(BF16)
    ups_next = jnp.where(lane == count - 1, 0.0, pltpu.roll(ups_t, count - 1, 1)).astype(BF16)
    sig_t, ups_t = sig_t.astype(BF16), ups_t.astype(BF16)
    for p in range(TOK):
        cut = CH * p
        for b in range(nblk):
            cols = slice(b * 128, b * 128 + 128)
            if p:
                lhs[pl.ds(b * 128, cut), pl.ds(p * 128, 128)] = sig_prev[128 - cut :, cols]
            lhs[pl.ds(b * 128 + cut, 128 - cut), pl.ds(p * 128, 128)] = sig_t[: 128 - cut, cols]
            size = count - 128 * b
            ahead[pl.ds(b * 128, 128 - cut), pl.ds(p * count, size)] = ups_t[cut:, b * 128 :]
            if p:
                ahead[pl.ds(b * 128 + 128 - cut, cut), pl.ds(p * count, size)] = ups_next[:cut, b * 128 :]
            if b:
                ahead[pl.ds(b * 128, 128), pl.ds(p * count + size, 128 * b)] = jnp.zeros((128, 128 * b), BF16)
    conv = [None] * nblk
    for b in range(nblk):
        rows = lhs[pl.ds(b * 128, 128), :]
        size = count - 128 * b
        part = jnp.dot(rows, hi_ref[:, pl.ds(0, size)], preferred_element_type=F32)
        part = part + jnp.dot(rows, lo_ref[:, pl.ds(0, size)], preferred_element_type=F32)
        for k in range(nblk - b):
            piece = part[:, k * 128 : k * 128 + 128]
            conv[b + k] = piece if conv[b + k] is None else conv[b + k] + piece
    back = jnp.dot(ahead[...], t_ref[...], preferred_element_type=F32)
    for b in range(nblk):
        rows = slice(b * 128, b * 128 + 128)
        wide[pl.ds(256 * b, 128, stride=2), :] = conv[b].T
        wide[pl.ds(256 * b + 1, 128, stride=2), :] = (back[rows, :128] + back[rows, 128:]).T
    o_ref[...] = wide[...].astype(BF16)
    side = jnp.concatenate([sig[b * 128 : b * 128 + 128] for b in range(nblk)], axis=1).astype(BF16)
    lane8, row8 = lane_of((8, count)), row_of((8, count))
    for p in range(TOK):
        lags = jnp.dot(side, ahead[:, pl.ds(p * count, count)], preferred_element_type=F32)
        total = jnp.zeros((8, count), F32)
        for r in range(ROWS // 8):
            part = jnp.where(lane8 >= row8 + 8 * r, lags[8 * r : 8 * r + 8], 0.0)
            total = total + (pltpu.roll(part, count - 8 * r, 1) if r else part)
        for bit in range(3):
            total = jnp.where((row8 >> bit) & 1 == 1, pltpu.roll(total, count - (1 << bit), 1), total)
        g_ref[pl.ds(p, 1), :] = jnp.sum(total, axis=0, keepdims=True)


def pack(query, key, value, grad):
    width = query.shape[1]
    rows = 2 * width // CH
    return pl.pallas_call(
        pack_kernel,
        out_shape=jax.ShapeDtypeStruct((rows, 128), BF16),
        scratch_shapes=[pltpu.VMEM((rows, 128), F32)],
        name="pack",
    )(query, key, value, grad)


def unpack(received, key, value, grad):
    shape = jax.ShapeDtypeStruct(key.shape, BF16)
    return pl.pallas_call(
        unpack_kernel,
        out_shape=(shape, shape, shape),
        scratch_shapes=[pltpu.VMEM(received.shape, F32)],
        name="unpack",
    )(received, key, value, grad)


def toeplitz(phases):
    width = phases.shape[1]
    return pl.pallas_call(
        toeplitz_kernel,
        out_shape=(
            jax.ShapeDtypeStruct((TOK * ROWS, width), BF16),
            jax.ShapeDtypeStruct((TOK * ROWS, width), BF16),
            jax.ShapeDtypeStruct((TOK * width, 2 * ROWS), BF16),
        ),
        scratch_shapes=[pltpu.VMEM((ROWS, width), F32)],
        name="toeplitz",
    )(phases)


def group(received, hi, lo, flipped):
    count = received.shape[0] // 2
    return pl.pallas_call(
        group_kernel,
        out_shape=(
            jax.ShapeDtypeStruct(received.shape, BF16),
            jax.ShapeDtypeStruct((TOK, count), F32),
        ),
        scratch_shapes=[
            pltpu.VMEM(received.shape, F32),
            pltpu.VMEM((count, TOK * ROWS), BF16),
            pltpu.VMEM((count, TOK * count), BF16),
        ],
        name="group",
    )(received, hi, lo, flipped)


def exchange(rows):
    pairs = rows.reshape(-1, 2, 128)
    return lax.all_to_all(pairs, ("ctx", "ch"), 0, 0, tiled=True).reshape(rows.shape)


def on_device(query_gate, key_gate, value_proj, grad_out, long_filters):
    groups, taps = long_filters.shape
    fine = taps // TOK
    by_phase = long_filters.reshape(groups, fine, TOK).transpose(0, 2, 1).reshape(groups, taps)
    own = lax.all_to_all(by_phase, "ctx", 0, 0, tiled=True)
    blocks = own.shape[0]
    phases = own.reshape(blocks, TOK, fine).transpose(1, 0, 2).reshape(TOK, blocks * fine)
    received = exchange(pack(query_gate, key_gate, value_proj, grad_out))
    hi, lo, flipped = toeplitz(phases)
    results, lags = group(received, hi, lo, flipped)
    by_block = lags.reshape(TOK, blocks, fine).transpose(1, 0, 2).reshape(blocks, taps)
    home = lax.all_to_all(by_block, "ctx", 0, 0, tiled=True)
    grad_filters = home.reshape(groups, TOK, fine).transpose(0, 2, 1).reshape(groups, taps)
    grads = unpack(exchange(results), key_gate, value_proj, grad_out)
    return (*grads, grad_filters)


def solution(mesh):
    tokens = P(("ctx", "ch"), None)
    return jax.shard_map(
        on_device,
        mesh=mesh,
        in_specs=(tokens, tokens, tokens, tokens, P("ch", "ctx")),
        out_specs=(tokens, tokens, tokens, P("ch", "ctx")),
        check_vma=False,
    )
```

```python
import jax
import jax.numpy as jnp
from jax import lax
from jax.experimental import pallas as pl
from jax.experimental.pallas import tpu as pltpu
from jax.sharding import Mesh
from jax.sharding import PartitionSpec as P

CH = 16
TOK = 8
ROWS = 128
NX, NZH, NCORE, NZL, NY = 4, 2, 2, 8, 4
NZ = NZH * NZL
NPLANE = NX * NCORE * NY
ZROWS = 2 * NPLANE + 8
PROWS = 2 * NZ + 8
Z_AXES = ("zh", "zl")
PLANE_AXES = ("x", "core", "y")
F32 = jnp.float32
BF16 = jnp.bfloat16


def lane_of(shape):
    return lax.broadcasted_iota(jnp.int32, shape, 1)


def row_of(shape):
    return lax.broadcasted_iota(jnp.int32, shape, 0)


def swap_segments(planes):
    planes = list(planes)
    seg = lane_of(planes[0].shape) // CH
    for bit in range(3):
        step = 1 << bit
        odd = (seg >> bit) & 1 == 1
        for low in range(TOK):
            if low & step:
                continue
            first, second = planes[low], planes[low + step]
            planes[low] = jnp.where(odd, pltpu.roll(second, CH * step, 1), first)
            planes[low + step] = jnp.where(odd, second, pltpu.roll(first, 128 - CH * step, 1))
    return planes


def phase_order(taps, back):
    shape = (taps, taps)
    source, target = row_of(shape), lane_of(shape)
    if back:
        source, target = target, source
    fine = taps // TOK
    return jnp.where((source % TOK) * fine + source // TOK == target, 1.0, 0.0).astype(BF16)


def halves(x):
    high = x.astype(BF16)
    return high, (x - high.astype(F32)).astype(BF16)


def pack_kernel(q_ref, k_ref, v_ref, g_ref, h_ref, o_ref, tile, wide):
    blocks = q_ref.shape[1] // 128
    for a, (x_ref, y_ref) in enumerate(((k_ref, v_ref), (g_ref, q_ref))):
        for block in range(blocks):
            lanes = pl.ds(block * 128, 128)
            prod = (x_ref[:, lanes].astype(F32) * y_ref[:, lanes].astype(F32)).astype(BF16)
            tile[a, pl.ds(block * TOK, TOK), :] = prod.astype(F32)
        for half in range(2):
            planes = [tile[a, pl.ds(half * TOK + t, blocks // 2, stride=2 * TOK), :] for t in range(TOK)]
            for i, plane in enumerate(swap_segments(planes)):
                wide[pl.ds((half * TOK + i) * ZROWS + a, blocks // 2, stride=2), :] = plane
    order = phase_order(h_ref.shape[1], False)
    for n, part in enumerate(halves(h_ref[...])):
        part = jnp.dot(part, order, preferred_element_type=F32)
        for n2 in range(2):
            wide[pl.ds(2 * NPLANE + 2 * n + n2, NZ, stride=ZROWS), :] = part[:, 128 * n2 : 128 * n2 + 128]
    for n in range(4, 8):
        wide[pl.ds(2 * NPLANE + n, NZ, stride=ZROWS), :] = jnp.zeros((NZ, 128), F32)
    o_ref[...] = wide[...].astype(BF16)


def inward_kernel(r_ref, o_ref, before, after):
    before[...] = r_ref[...].astype(F32)
    for j in range(NPLANE):
        for a in range(2):
            after[pl.ds(PROWS * j + a, NZ, stride=2), :] = before[pl.ds(2 * j + a, NZ, stride=ZROWS), :]
    for zl in range(NZL):
        parts = [before[pl.ds((zh * NZL + zl) * ZROWS + 2 * NPLANE, 4), :] for zh in range(NZH)]
        block = jnp.concatenate(parts, axis=0)
        for y in range(NY):
            after[pl.ds((zl * NY + y) * PROWS + 2 * NZ, 8), :] = block
    o_ref[...] = after[...].astype(BF16)


def outward_kernel(y_ref, r_ref, o_ref, before, after):
    before[...] = r_ref[...].astype(F32)
    for j in range(NPLANE):
        for a in range(2):
            after[pl.ds(2 * j + a, NZ, stride=ZROWS), :] = before[pl.ds(PROWS * j + a, NZ, stride=2), :]
    for zl in range(NZL):
        at = pl.multiple_of((zl * NY + y_ref[0]) * PROWS + 2 * NZ, 8)
        block = before[pl.ds(at, 8), :]
        after[pl.ds(zl * ZROWS + 2 * NPLANE, 8), :] = block
        after[pl.ds((NZL + zl) * ZROWS + 2 * NPLANE, 8), :] = pltpu.roll(block, 4, 0)
    o_ref[...] = after[...].astype(BF16)


def unpack_kernel(r_ref, k_ref, v_ref, g_ref, gq_ref, gk_ref, gv_ref, gh_ref, tile, wide):
    blocks = k_ref.shape[1] // 128
    wide[...] = r_ref[...].astype(F32)
    for a in range(2):
        for half in range(2):
            planes = [
                wide[pl.ds((half * TOK + i) * ZROWS + a, blocks // 2, stride=2), :] for i in range(TOK)
            ]
            for t, plane in enumerate(swap_segments(planes)):
                tile[a, pl.ds(half * TOK + t, blocks // 2, stride=2 * TOK), :] = plane
    for block in range(blocks):
        lanes = pl.ds(block * 128, 128)
        conv = tile[0, pl.ds(block * TOK, TOK), :]
        corr = tile[1, pl.ds(block * TOK, TOK), :]
        gq_ref[:, lanes] = (g_ref[:, lanes].astype(F32) * conv).astype(BF16)
        gk_ref[:, lanes] = (corr * v_ref[:, lanes].astype(F32)).astype(BF16)
        gv_ref[:, lanes] = (corr * k_ref[:, lanes].astype(F32)).astype(BF16)
    order = phase_order(gh_ref.shape[1], True)
    total = None
    for n in range(2):
        rows = [wide[pl.ds(2 * NPLANE + 2 * n + n2, NZ, stride=ZROWS), :] for n2 in range(2)]
        part = jnp.dot(jnp.concatenate(rows, axis=1).astype(BF16), order, preferred_element_type=F32)
        total = part if total is None else total + part
    gh_ref[...] = total


def columns(x):
    return jnp.concatenate([x[b : b + 128].T for b in range(0, x.shape[0], 128)], axis=1)


def row_pieces():
    for x in range(NX):
        for zh in range(NZH):
            for core in range(NCORE):
                for y in range(NY):
                    q = (((x * NZH + zh) * NCORE + core) * NZL) * NY + y
                    sent = ((x * NCORE + core) * NY + y) * PROWS + 2 * NZL * zh
                    yield q, sent


def read_taps(y, wide):
    shape = (TOK, 128)
    row, seg = row_of(shape), lane_of(shape) // 32
    out = []
    for x in range(NX):
        column = jnp.zeros(shape, F32)
        for core in range(NCORE):
            at = pl.multiple_of(((x * NCORE + core) * NY + y) * PROWS + 2 * NZ, 8)
            got = wide[pl.ds(at, 8), :]
            for zh in range(NZH):
                low, high = (got[4 * zh + n : 4 * zh + n + 1] + got[4 * zh + n + 2 : 4 * zh + n + 3] for n in range(2))
                both = jnp.where(row < 4, low, high)
                place = zh * NCORE + core
                for d in range(4):
                    moved = pltpu.roll(both, 32 * ((place - d) % 4), 1) if place != d else both
                    column = jnp.where((seg == place) & (row % 4 == d), moved, column)
        out.append(column)
    return jnp.concatenate(out, axis=1)


def write_lags(lags, wide):
    shape = (TOK, 128)
    row, seg = row_of(shape), lane_of(shape) // 32
    for x in range(NX):
        column = lags[:, x * 128 : x * 128 + 128]
        for core in range(NCORE):
            rows = []
            for zh in range(NZH):
                place = zh * NCORE + core
                spread = jnp.zeros(shape, F32)
                for d in range(4):
                    moved = pltpu.roll(column, 32 * ((d - place) % 4), 1) if place != d else column
                    spread = jnp.where((seg == d) & (row % 4 == d), moved, spread)
                pair = [jnp.sum(spread[4 * n : 4 * n + 4], axis=0, keepdims=True) for n in range(2)]
                high = [value.astype(BF16).astype(F32) for value in pair]
                rows += high + [value - h for value, h in zip(pair, high)]
            block = jnp.concatenate(rows, axis=0)
            for y in range(NY):
                wide[pl.ds(((x * NCORE + core) * NY + y) * PROWS + 2 * NZ, 8), :] = block


def group_kernel(y_ref, r_ref, o_ref, wide, rows, lhs, ahead, base, hi, lo, flipped):
    count = rows.shape[1]
    nblk = count // ROWS
    lane8, row8 = lane_of((TOK, count)), row_of((TOK, count))
    wide[...] = r_ref[...].astype(F32)
    taps = read_taps(y_ref[0], wide)
    for p in range(TOK):
        skew = jnp.broadcast_to(taps[p : p + 1], (TOK, count))
        for bit in range(3):
            skew = jnp.where((row8 >> bit) & 1 == 1, pltpu.roll(skew, 1 << bit, 1), skew)
        for r in range(ROWS // 8):
            part = pltpu.roll(skew, 8 * r, 1) if r else skew
            base[pl.ds(8 * r, 8), :] = jnp.where(lane8 >= row8 + 8 * r, part, 0.0)
        whole = base[...]
        hi[pl.ds(p * ROWS, ROWS), :], lo[pl.ds(p * ROWS, ROWS), :] = halves(whole)
        for m in range(nblk):
            at = pl.ds(p * count + m * 128, 128)
            flipped[at, pl.ds(0, 128)], flipped[at, pl.ds(128, 128)] = halves(whole[:, m * 128 : (m + 1) * 128].T)
    for q, sent in row_pieces():
        for a in range(2):
            rows[a, pl.ds(q, NZL, stride=NY), :] = wide[pl.ds(sent + a, NZL, stride=2), :]
    sig, ups = rows[0], rows[1]
    sig_t, ups_t = columns(sig), columns(ups)
    lane = lane_of(sig_t.shape)
    sig_prev = jnp.where(lane == 0, 0.0, pltpu.roll(sig_t, 1, 1)).astype(BF16)
    ups_next = jnp.where(lane == count - 1, 0.0, pltpu.roll(ups_t, count - 1, 1)).astype(BF16)
    sig_t, ups_t = sig_t.astype(BF16), ups_t.astype(BF16)
    for p in range(TOK):
        cut = CH * p
        for b in range(nblk):
            cols = slice(b * 128, b * 128 + 128)
            if p:
                lhs[pl.ds(b * 128, cut), pl.ds(p * 128, 128)] = sig_prev[128 - cut :, cols]
            lhs[pl.ds(b * 128 + cut, 128 - cut), pl.ds(p * 128, 128)] = sig_t[: 128 - cut, cols]
            size = count - 128 * b
            ahead[pl.ds(b * 128, 128 - cut), pl.ds(p * count, size)] = ups_t[cut:, b * 128 :]
            if p:
                ahead[pl.ds(b * 128 + 128 - cut, cut), pl.ds(p * count, size)] = ups_next[:cut, b * 128 :]
            if b:
                ahead[pl.ds(b * 128, 128), pl.ds(p * count + size, 128 * b)] = jnp.zeros((128, 128 * b), BF16)
    side = jnp.concatenate([sig[b * 128 : b * 128 + 128] for b in range(nblk)], axis=1).astype(BF16)
    sums = []
    for p in range(TOK):
        lags = jnp.dot(side, ahead[:, pl.ds(p * count, count)], preferred_element_type=F32)
        total = jnp.zeros((TOK, count), F32)
        for r in range(ROWS // 8):
            part = jnp.where(lane8 >= row8 + 8 * r, lags[8 * r : 8 * r + 8], 0.0)
            total = total + (pltpu.roll(part, count - 8 * r, 1) if r else part)
        for bit in range(3):
            total = jnp.where((row8 >> bit) & 1 == 1, pltpu.roll(total, count - (1 << bit), 1), total)
        sums.append(jnp.sum(total, axis=0, keepdims=True))
    write_lags(jnp.concatenate(sums, axis=0), wide)
    conv = [None] * nblk
    for b in range(nblk):
        block = lhs[pl.ds(b * 128, 128), :]
        size = count - 128 * b
        part = jnp.dot(block, hi[:, pl.ds(0, size)], preferred_element_type=F32)
        part = part + jnp.dot(block, lo[:, pl.ds(0, size)], preferred_element_type=F32)
        for k in range(nblk - b):
            piece = part[:, k * 128 : k * 128 + 128]
            conv[b + k] = piece if conv[b + k] is None else conv[b + k] + piece
    back = jnp.dot(ahead[...], flipped[...], preferred_element_type=F32)
    for b in range(nblk):
        at = pl.ds(b * 128, 128)
        rows[0, at, :] = conv[b].T
        rows[1, at, :] = (back[b * 128 : b * 128 + 128, :128] + back[b * 128 : b * 128 + 128, 128:]).T
    for q, sent in row_pieces():
        for a in range(2):
            wide[pl.ds(sent + a, NZL, stride=2), :] = rows[a, pl.ds(q, NZL, stride=NY), :]
    o_ref[...] = wide[...].astype(BF16)


def params(mib):
    return pltpu.CompilerParams(vmem_limit_bytes=mib << 20)


def pack(query, key, value, grad, filters):
    rows = query.shape[1] // CH
    return pl.pallas_call(
        pack_kernel,
        out_shape=jax.ShapeDtypeStruct((NZ * ZROWS, 128), BF16),
        scratch_shapes=[pltpu.VMEM((2, rows, 128), F32), pltpu.VMEM((NZ * ZROWS, 128), F32)],
        compiler_params=params(8),
        name="pack",
    )(query, key, value, grad, filters)


def unpack(received, key, value, grad, filters):
    shape = jax.ShapeDtypeStruct(key.shape, BF16)
    rows = key.shape[1] // CH
    return pl.pallas_call(
        unpack_kernel,
        out_shape=(shape, shape, shape, jax.ShapeDtypeStruct(filters.shape, F32)),
        scratch_shapes=[pltpu.VMEM((2, rows, 128), F32), pltpu.VMEM((NZ * ZROWS, 128), F32)],
        compiler_params=params(8),
        name="unpack",
    )(received, key, value, grad)


def inward(received):
    return pl.pallas_call(
        inward_kernel,
        out_shape=jax.ShapeDtypeStruct((NPLANE * PROWS, 128), BF16),
        scratch_shapes=[pltpu.VMEM((NZ * ZROWS, 128), F32), pltpu.VMEM((NPLANE * PROWS, 128), F32)],
        compiler_params=params(8),
        name="inward",
    )(received)


def outward(y, received):
    return pl.pallas_call(
        outward_kernel,
        out_shape=jax.ShapeDtypeStruct((NZ * ZROWS, 128), BF16),
        in_specs=[pl.BlockSpec(memory_space=pltpu.SMEM), pl.BlockSpec(memory_space=pltpu.VMEM)],
        scratch_shapes=[pltpu.VMEM((NPLANE * PROWS, 128), F32), pltpu.VMEM((NZ * ZROWS, 128), F32)],
        compiler_params=params(8),
        name="outward",
    )(y, received)


def group(y, received):
    count = NZ * NPLANE
    return pl.pallas_call(
        group_kernel,
        out_shape=jax.ShapeDtypeStruct(received.shape, BF16),
        in_specs=[pl.BlockSpec(memory_space=pltpu.SMEM), pl.BlockSpec(memory_space=pltpu.VMEM)],
        scratch_shapes=[
            pltpu.VMEM(received.shape, F32),
            pltpu.VMEM((2, count, 128), F32),
            pltpu.VMEM((count, TOK * ROWS), BF16),
            pltpu.VMEM((count, TOK * count), BF16),
            pltpu.VMEM((ROWS, count), F32),
            pltpu.VMEM((TOK * ROWS, count), BF16),
            pltpu.VMEM((TOK * ROWS, count), BF16),
            pltpu.VMEM((TOK * count, 2 * ROWS), BF16),
        ],
        compiler_params=params(32),
        name="group",
    )(y, received)


def exchange(rows, axes, parts):
    chunks = rows.reshape(parts, rows.shape[0] // parts, 128)
    return lax.all_to_all(chunks, axes, 0, 0, tiled=True).reshape(rows.shape)


def on_device(query_gate, key_gate, value_proj, grad_out, long_filters):
    y = lax.axis_index("y").astype(jnp.int32).reshape(1)
    rows = pack(query_gate, key_gate, value_proj, grad_out, long_filters)
    rows = inward(exchange(rows, Z_AXES, NZ))
    rows = group(y, exchange(rows, PLANE_AXES, NPLANE))
    rows = outward(y, exchange(rows, PLANE_AXES, NPLANE))
    return unpack(exchange(rows, Z_AXES, NZ), key_gate, value_proj, grad_out, long_filters)


def solution(mesh):
    fine = Mesh(mesh.devices.reshape(NX, NZH, NCORE, NZL, NY), ("x", "zh", "core", "zl", "y"))
    tokens = P(("x", "zh", "core", "zl", "y"), None)
    filters = P(("zl", "y"), ("x", "zh", "core"))
    return jax.shard_map(
        on_device,
        mesh=fine,
        in_specs=(tokens, tokens, tokens, tokens, filters),
        out_specs=(tokens, tokens, tokens, filters),
        check_vma=False,
    )
```

```python
import jax
import jax.numpy as jnp
from jax import lax
from jax.experimental import pallas as pl
from jax.experimental.pallas import tpu as pltpu
from jax.sharding import Mesh
from jax.sharding import PartitionSpec as P

CH = 16
TOK = 8
ROWS = 128
NX, NZH, NCORE, NZL, NY = 4, 2, 2, 8, 4
NZ = NZH * NZL
NPLANE = NX * NCORE * NY
ZROWS = 2 * NPLANE + 4
PROWS = 2 * NZ + 8
Z_AXES = ("zh", "zl")
PLANE_AXES = ("x", "core", "y")
F32 = jnp.float32
BF16 = jnp.bfloat16


def lane_of(shape):
    return lax.broadcasted_iota(jnp.int32, shape, 1)


def row_of(shape):
    return lax.broadcasted_iota(jnp.int32, shape, 0)


def swap_segments(planes):
    planes = list(planes)
    seg = lane_of(planes[0].shape) // CH
    for bit in range(3):
        step = 1 << bit
        odd = (seg >> bit) & 1 == 1
        for low in range(TOK):
            if low & step:
                continue
            first, second = planes[low], planes[low + step]
            planes[low] = jnp.where(odd, pltpu.roll(second, CH * step, 1), first)
            planes[low + step] = jnp.where(odd, second, pltpu.roll(first, 128 - CH * step, 1))
    return planes


def phase_order(taps, back):
    shape = (taps, taps)
    source, target = row_of(shape), lane_of(shape)
    if back:
        source, target = target, source
    fine = taps // TOK
    return jnp.where((source % TOK) * fine + source // TOK == target, 1.0, 0.0).astype(BF16)


def halves(x):
    high = x.astype(BF16)
    return high, (x - high.astype(F32)).astype(BF16)


def pack_kernel(k_hbm, v_hbm, g_hbm, q_hbm, h_hbm, o_ref, inputs, taps, tile, wide, sems):
    copies = [
        pltpu.make_async_copy(hbm, inputs.at[n], sems.at[n]) for n, hbm in enumerate((k_hbm, v_hbm, g_hbm, q_hbm))
    ]
    copies.append(pltpu.make_async_copy(h_hbm, taps, sems.at[4]))
    for copy in copies[4:] + copies[:4]:
        copy.start()
    order = phase_order(taps.shape[1], False)
    copies[4].wait()
    for n, part in enumerate(halves(taps[...])):
        part = jnp.dot(part, order, preferred_element_type=F32)
        for n2 in range(2):
            wide[pl.ds(2 * NPLANE + 2 * n + n2, NZ, stride=ZROWS), :] = part[:, 128 * n2 : 128 * n2 + 128]
    blocks = k_hbm.shape[1] // 128
    for a in range(2):
        copies[2 * a].wait()
        copies[2 * a + 1].wait()
        for block in range(blocks):
            lanes = pl.ds(block * 128, 128)
            prod = (inputs[2 * a, :, lanes].astype(F32) * inputs[2 * a + 1, :, lanes].astype(F32)).astype(BF16)
            tile[a, pl.ds(block * TOK, TOK), :] = prod.astype(F32)
        for half in range(2):
            planes = [tile[a, pl.ds(half * TOK + t, blocks // 2, stride=2 * TOK), :] for t in range(TOK)]
            for i, plane in enumerate(swap_segments(planes)):
                wide[pl.ds((half * TOK + i) * ZROWS + a, blocks // 2, stride=2), :] = plane
    o_ref[...] = wide[...].astype(BF16)


def inward_kernel(r_ref, o_ref, before, after):
    before[...] = r_ref[...].astype(F32)
    for j in range(NPLANE):
        for a in range(2):
            after[pl.ds(PROWS * j + a, NZ, stride=2), :] = before[pl.ds(2 * j + a, NZ, stride=ZROWS), :]
    for zl in range(NZL):
        parts = [before[pl.ds((zh * NZL + zl) * ZROWS + 2 * NPLANE, 4), :] for zh in range(NZH)]
        block = jnp.concatenate(parts, axis=0)
        for y in range(NY):
            after[pl.ds((zl * NY + y) * PROWS + 2 * NZ, 8), :] = block
    o_ref[...] = after[...].astype(BF16)


def outward_kernel(r_ref, o_ref, before, after):
    own = lax.axis_index("y")
    before[...] = r_ref[...].astype(F32)
    for j in range(NPLANE):
        for a in range(2):
            after[pl.ds(2 * j + a, NZ, stride=ZROWS), :] = before[pl.ds(PROWS * j + a, NZ, stride=2), :]
    for zl in range(NZL):
        at = pl.multiple_of((zl * NY + own) * PROWS + 2 * NZ, 8)
        block = before[pl.ds(at, 8), :]
        for zh in range(NZH):
            after[pl.ds((zh * NZL + zl) * ZROWS + 2 * NPLANE, 4), :] = block[4 * zh : 4 * zh + 4]
    o_ref[...] = after[...].astype(BF16)


def unpack_kernel(r_ref, k_ref, v_ref, g_ref, gq_hbm, gk_hbm, gv_hbm, gh_ref, results, tile, wide, sems):
    blocks = k_ref.shape[1] // 128
    copies = [
        pltpu.make_async_copy(results.at[n], hbm, sems.at[n]) for n, hbm in enumerate((gq_hbm, gk_hbm, gv_hbm))
    ]
    wide[...] = r_ref[...].astype(F32)
    for a in range(2):
        for half in range(2):
            planes = [
                wide[pl.ds((half * TOK + i) * ZROWS + a, blocks // 2, stride=2), :] for i in range(TOK)
            ]
            for t, plane in enumerate(swap_segments(planes)):
                tile[a, pl.ds(half * TOK + t, blocks // 2, stride=2 * TOK), :] = plane
        for n, gate in enumerate((v_ref, k_ref) if a else (g_ref,)):
            for block in range(blocks):
                lanes = pl.ds(block * 128, 128)
                value = gate[:, lanes].astype(F32) * tile[a, pl.ds(block * TOK, TOK), :]
                results[a + n, :, lanes] = value.astype(BF16)
            copies[a + n].start()
    order = phase_order(gh_ref.shape[1], True)
    total = None
    for n in range(2):
        rows = [wide[pl.ds(2 * NPLANE + 2 * n + n2, NZ, stride=ZROWS), :] for n2 in range(2)]
        part = jnp.dot(jnp.concatenate(rows, axis=1).astype(BF16), order, preferred_element_type=F32)
        total = part if total is None else total + part
    gh_ref[...] = total
    for copy in copies:
        copy.wait()


def columns(x):
    return jnp.concatenate([x[b : b + 128].T for b in range(0, x.shape[0], 128)], axis=1)


def row_pieces():
    for x in range(NX):
        for zh in range(NZH):
            for core in range(NCORE):
                for y in range(NY):
                    q = (((x * NZH + zh) * NCORE + core) * NZL) * NY + y
                    sent = ((x * NCORE + core) * NY + y) * PROWS + 2 * NZL * zh
                    yield q, sent


def read_taps(y, wide):
    shape = (TOK, 128)
    row, seg = row_of(shape), lane_of(shape) // 32
    out = []
    for x in range(NX):
        column = jnp.zeros(shape, F32)
        for core in range(NCORE):
            at = pl.multiple_of(((x * NCORE + core) * NY + y) * PROWS + 2 * NZ, 8)
            got = wide[pl.ds(at, 8), :]
            for zh in range(NZH):
                low, high = (got[4 * zh + n : 4 * zh + n + 1] + got[4 * zh + n + 2 : 4 * zh + n + 3] for n in range(2))
                both = jnp.where(row < 4, low, high)
                place = zh * NCORE + core
                for d in range(4):
                    moved = pltpu.roll(both, 32 * ((place - d) % 4), 1) if place != d else both
                    column = jnp.where((seg == place) & (row % 4 == d), moved, column)
        out.append(column)
    return jnp.concatenate(out, axis=1)


def write_lags(lags, wide):
    shape = (TOK, 128)
    row, seg = row_of(shape), lane_of(shape) // 32
    for x in range(NX):
        column = lags[:, x * 128 : x * 128 + 128]
        for core in range(NCORE):
            rows = []
            for zh in range(NZH):
                place = zh * NCORE + core
                spread = jnp.zeros(shape, F32)
                for d in range(4):
                    moved = pltpu.roll(column, 32 * ((d - place) % 4), 1) if place != d else column
                    spread = jnp.where((seg == d) & (row % 4 == d), moved, spread)
                pair = [jnp.sum(spread[4 * n : 4 * n + 4], axis=0, keepdims=True) for n in range(2)]
                high = [value.astype(BF16).astype(F32) for value in pair]
                rows += high + [value - h for value, h in zip(pair, high)]
            block = jnp.concatenate(rows, axis=0)
            for y in range(NY):
                wide[pl.ds(((x * NCORE + core) * NY + y) * PROWS + 2 * NZ, 8), :] = block


def group_kernel(r_ref, o_ref, wide, rows, lhs, ahead, base, hi, lo, flipped):
    count = rows.shape[1]
    nblk = count // ROWS
    lane8, row8 = lane_of((TOK, count)), row_of((TOK, count))
    wide[...] = r_ref[...].astype(F32)
    taps = read_taps(lax.axis_index("y"), wide)
    for p in range(TOK):
        skew = jnp.broadcast_to(taps[p : p + 1], (TOK, count))
        for bit in range(3):
            skew = jnp.where((row8 >> bit) & 1 == 1, pltpu.roll(skew, 1 << bit, 1), skew)
        for r in range(ROWS // 8):
            part = pltpu.roll(skew, 8 * r, 1) if r else skew
            base[pl.ds(8 * r, 8), :] = jnp.where(lane8 >= row8 + 8 * r, part, 0.0)
        whole = base[...]
        hi[pl.ds(p * ROWS, ROWS), :], lo[pl.ds(p * ROWS, ROWS), :] = halves(whole)
        for m in range(nblk):
            at = pl.ds(p * count + m * 128, 128)
            flipped[at, pl.ds(0, 128)], flipped[at, pl.ds(128, 128)] = halves(whole[:, m * 128 : (m + 1) * 128].T)
    for q, sent in row_pieces():
        for a in range(2):
            rows[a, pl.ds(q, NZL, stride=NY), :] = wide[pl.ds(sent + a, NZL, stride=2), :]
    sig, ups = rows[0], rows[1]
    sig_t, ups_t = columns(sig), columns(ups)
    lane = lane_of(sig_t.shape)
    sig_prev = jnp.where(lane == 0, 0.0, pltpu.roll(sig_t, 1, 1)).astype(BF16)
    ups_next = jnp.where(lane == count - 1, 0.0, pltpu.roll(ups_t, count - 1, 1)).astype(BF16)
    sig_t, ups_t = sig_t.astype(BF16), ups_t.astype(BF16)
    for p in range(TOK):
        cut = CH * p
        for b in range(nblk):
            cols = slice(b * 128, b * 128 + 128)
            if p:
                lhs[pl.ds(b * 128, cut), pl.ds(p * 128, 128)] = sig_prev[128 - cut :, cols]
            lhs[pl.ds(b * 128 + cut, 128 - cut), pl.ds(p * 128, 128)] = sig_t[: 128 - cut, cols]
            size = count - 128 * b
            ahead[pl.ds(b * 128, 128 - cut), pl.ds(p * count, size)] = ups_t[cut:, b * 128 :]
            if p:
                ahead[pl.ds(b * 128 + 128 - cut, cut), pl.ds(p * count, size)] = ups_next[:cut, b * 128 :]
            if b:
                ahead[pl.ds(b * 128, 128), pl.ds(p * count + size, 128 * b)] = jnp.zeros((128, 128 * b), BF16)
    side = jnp.concatenate([sig[b * 128 : b * 128 + 128] for b in range(nblk)], axis=1).astype(BF16)
    sums = []
    for p in range(TOK):
        lags = jnp.dot(side, ahead[:, pl.ds(p * count, count)], preferred_element_type=F32)
        total = jnp.zeros((TOK, count), F32)
        for r in range(ROWS // 8):
            part = jnp.where(lane8 >= row8 + 8 * r, lags[8 * r : 8 * r + 8], 0.0)
            total = total + (pltpu.roll(part, count - 8 * r, 1) if r else part)
        for bit in range(3):
            total = jnp.where((row8 >> bit) & 1 == 1, pltpu.roll(total, count - (1 << bit), 1), total)
        sums.append(jnp.sum(total, axis=0, keepdims=True))
    write_lags(jnp.concatenate(sums, axis=0), wide)
    conv = [None] * nblk
    for b in range(nblk):
        block = lhs[pl.ds(b * 128, 128), :]
        size = count - 128 * b
        part = jnp.dot(block, hi[:, pl.ds(0, size)], preferred_element_type=F32)
        part = part + jnp.dot(block, lo[:, pl.ds(0, size)], preferred_element_type=F32)
        for k in range(nblk - b):
            piece = part[:, k * 128 : k * 128 + 128]
            conv[b + k] = piece if conv[b + k] is None else conv[b + k] + piece
    back = jnp.dot(ahead[...], flipped[...], preferred_element_type=F32)
    for b in range(nblk):
        at = pl.ds(b * 128, 128)
        rows[0, at, :] = conv[b].T
        rows[1, at, :] = (back[b * 128 : b * 128 + 128, :128] + back[b * 128 : b * 128 + 128, 128:]).T
    for q, sent in row_pieces():
        for a in range(2):
            wide[pl.ds(sent + a, NZL, stride=2), :] = rows[a, pl.ds(q, NZL, stride=NY), :]
    o_ref[...] = wide[...].astype(BF16)


def params(mib):
    return pltpu.CompilerParams(vmem_limit_bytes=mib << 20)


def pack(query, key, value, grad, filters):
    rows = query.shape[1] // CH
    return pl.pallas_call(
        pack_kernel,
        out_shape=jax.ShapeDtypeStruct((NZ * ZROWS, 128), BF16),
        in_specs=[pl.BlockSpec(memory_space=pltpu.HBM)] * 5,
        scratch_shapes=[
            pltpu.VMEM((4, *query.shape), BF16),
            pltpu.VMEM(filters.shape, F32),
            pltpu.VMEM((2, rows, 128), F32),
            pltpu.VMEM((NZ * ZROWS, 128), F32),
            pltpu.SemaphoreType.DMA((5,)),
        ],
        compiler_params=params(8),
        name="pack",
    )(*(pltpu.with_memory_space_constraint(x, pltpu.HBM) for x in (key, value, grad, query, filters)))


def unpack(received, key, value, grad, filters):
    shape = jax.ShapeDtypeStruct(key.shape, BF16)
    rows = key.shape[1] // CH
    return pl.pallas_call(
        unpack_kernel,
        out_shape=(shape, shape, shape, jax.ShapeDtypeStruct(filters.shape, F32)),
        out_specs=[pl.BlockSpec(memory_space=pltpu.HBM)] * 3 + [pl.BlockSpec(memory_space=pltpu.VMEM)],
        scratch_shapes=[
            pltpu.VMEM((3, *key.shape), BF16),
            pltpu.VMEM((2, rows, 128), F32),
            pltpu.VMEM((NZ * ZROWS, 128), F32),
            pltpu.SemaphoreType.DMA((3,)),
        ],
        compiler_params=params(8),
        name="unpack",
    )(received, key, value, grad)


def inward(received):
    return pl.pallas_call(
        inward_kernel,
        out_shape=jax.ShapeDtypeStruct((NPLANE * PROWS, 128), BF16),
        scratch_shapes=[pltpu.VMEM((NZ * ZROWS, 128), F32), pltpu.VMEM((NPLANE * PROWS, 128), F32)],
        compiler_params=params(8),
        name="inward",
    )(received)


def outward(received):
    return pl.pallas_call(
        outward_kernel,
        out_shape=jax.ShapeDtypeStruct((NZ * ZROWS, 128), BF16),
        scratch_shapes=[pltpu.VMEM((NPLANE * PROWS, 128), F32), pltpu.VMEM((NZ * ZROWS, 128), F32)],
        compiler_params=params(8),
        name="outward",
    )(received)


def group(received):
    count = NZ * NPLANE
    return pl.pallas_call(
        group_kernel,
        out_shape=jax.ShapeDtypeStruct(received.shape, BF16),
        scratch_shapes=[
            pltpu.VMEM(received.shape, F32),
            pltpu.VMEM((2, count, 128), F32),
            pltpu.VMEM((count, TOK * ROWS), BF16),
            pltpu.VMEM((count, TOK * count), BF16),
            pltpu.VMEM((ROWS, count), F32),
            pltpu.VMEM((TOK * ROWS, count), BF16),
            pltpu.VMEM((TOK * ROWS, count), BF16),
            pltpu.VMEM((TOK * count, 2 * ROWS), BF16),
        ],
        compiler_params=params(32),
        name="group",
    )(received)


def exchange(rows, axes):
    chunks = rows.reshape(-1, 4, 128)
    return lax.all_to_all(chunks, axes, 0, 0, tiled=True).reshape(rows.shape)


def on_device(query_gate, key_gate, value_proj, grad_out, long_filters):
    rows = pack(query_gate, key_gate, value_proj, grad_out, long_filters)
    rows = inward(exchange(rows, Z_AXES))
    rows = group(exchange(rows, PLANE_AXES))
    rows = outward(exchange(rows, PLANE_AXES))
    return unpack(exchange(rows, Z_AXES), key_gate, value_proj, grad_out, long_filters)


def solution(mesh):
    fine = Mesh(mesh.devices.reshape(NX, NZH, NCORE, NZL, NY), ("x", "zh", "core", "zl", "y"))
    tokens = P(("x", "zh", "core", "zl", "y"), None)
    filters = P(("zl", "y"), ("x", "zh", "core"))
    return jax.shard_map(
        on_device,
        mesh=fine,
        in_specs=(tokens, tokens, tokens, tokens, filters),
        out_specs=(tokens, tokens, tokens, filters),
        check_vma=False,
    )
```

```python
import jax
import jax.numpy as jnp
from jax import lax
from jax.experimental import pallas as pl
from jax.experimental.pallas import tpu as pltpu
from jax.sharding import Mesh
from jax.sharding import PartitionSpec as P

CH = 16
TOK = 8
ROWS = 128
NX, NZH, NCORE, NZL, NY = 4, 2, 2, 8, 4
NZ = NZH * NZL
NPLANE = NX * NCORE * NY
ZROWS = 2 * NPLANE + 4
PROWS = 2 * NZ + 8
Z_AXES = ("zh", "zl")
PLANE_AXES = ("x", "core", "y")
F32 = jnp.float32
BF16 = jnp.bfloat16


def lane_of(shape):
    return lax.broadcasted_iota(jnp.int32, shape, 1)


def row_of(shape):
    return lax.broadcasted_iota(jnp.int32, shape, 0)


def swap_segments(planes):
    planes = list(planes)
    seg = lane_of(planes[0].shape) // CH
    for bit in range(3):
        step = 1 << bit
        odd = (seg >> bit) & 1 == 1
        for low in range(TOK):
            if low & step:
                continue
            first, second = planes[low], planes[low + step]
            planes[low] = jnp.where(odd, pltpu.roll(second, CH * step, 1), first)
            planes[low + step] = jnp.where(odd, second, pltpu.roll(first, 128 - CH * step, 1))
    return planes


def phase_order(taps, back):
    shape = (taps, taps)
    source, target = row_of(shape), lane_of(shape)
    if back:
        source, target = target, source
    fine = taps // TOK
    return jnp.where((source % TOK) * fine + source // TOK == target, 1.0, 0.0).astype(BF16)


def halves(x):
    high = x.astype(BF16)
    return high, (x - high.astype(F32)).astype(BF16)


def pack_kernel(k_hbm, v_hbm, g_hbm, q_hbm, h_hbm, o_ref, inputs, taps, tile, wide, sems):
    copies = [
        pltpu.make_async_copy(hbm, inputs.at[n], sems.at[n]) for n, hbm in enumerate((k_hbm, v_hbm, g_hbm, q_hbm))
    ]
    copies.append(pltpu.make_async_copy(h_hbm, taps, sems.at[4]))
    for copy in copies[4:] + copies[:4]:
        copy.start()
    order = phase_order(taps.shape[1], False)
    copies[4].wait()
    for n, part in enumerate(halves(taps[...])):
        part = jnp.dot(part, order, preferred_element_type=F32)
        for n2 in range(2):
            wide[pl.ds(2 * NPLANE + 2 * n + n2, NZ, stride=ZROWS), :] = part[:, 128 * n2 : 128 * n2 + 128]
    blocks = k_hbm.shape[1] // 128
    for a in range(2):
        copies[2 * a].wait()
        copies[2 * a + 1].wait()
        for block in range(blocks):
            lanes = pl.ds(block * 128, 128)
            prod = (inputs[2 * a, :, lanes].astype(F32) * inputs[2 * a + 1, :, lanes].astype(F32)).astype(BF16)
            tile[a, pl.ds(block * TOK, TOK), :] = prod.astype(F32)
        for half in range(2):
            planes = [tile[a, pl.ds(half * TOK + t, blocks // 2, stride=2 * TOK), :] for t in range(TOK)]
            for i, plane in enumerate(swap_segments(planes)):
                wide[pl.ds((half * TOK + i) * ZROWS + a, blocks // 2, stride=2), :] = plane
    o_ref[...] = wide[...].astype(BF16)


def inward_kernel(r_ref, o_ref, before, after):
    before[...] = r_ref[...].astype(F32)
    for j in range(NPLANE):
        for a in range(2):
            after[pl.ds(PROWS * j + a, NZ, stride=2), :] = before[pl.ds(2 * j + a, NZ, stride=ZROWS), :]
    for zl in range(NZL):
        parts = [before[pl.ds((zh * NZL + zl) * ZROWS + 2 * NPLANE, 4), :] for zh in range(NZH)]
        block = jnp.concatenate(parts, axis=0)
        for y in range(NY):
            after[pl.ds((zl * NY + y) * PROWS + 2 * NZ, 8), :] = block
    o_ref[...] = after[...].astype(BF16)


def outward_kernel(r_ref, o_ref, before, after):
    own = lax.axis_index("y")
    before[...] = r_ref[...].astype(F32)
    for j in range(NPLANE):
        for a in range(2):
            after[pl.ds(2 * j + a, NZ, stride=ZROWS), :] = before[pl.ds(PROWS * j + a, NZ, stride=2), :]
    for zl in range(NZL):
        at = pl.multiple_of((zl * NY + own) * PROWS + 2 * NZ, 8)
        block = before[pl.ds(at, 8), :]
        for zh in range(NZH):
            after[pl.ds((zh * NZL + zl) * ZROWS + 2 * NPLANE, 4), :] = block[4 * zh : 4 * zh + 4]
    o_ref[...] = after[...].astype(BF16)


def unpack_kernel(r_ref, k_ref, v_ref, g_ref, gq_ref, gk_ref, gv_ref, gh_ref, tile, wide):
    blocks = k_ref.shape[1] // 128
    wide[...] = r_ref[...].astype(F32)
    for a in range(2):
        for half in range(2):
            planes = [
                wide[pl.ds((half * TOK + i) * ZROWS + a, blocks // 2, stride=2), :] for i in range(TOK)
            ]
            for t, plane in enumerate(swap_segments(planes)):
                tile[a, pl.ds(half * TOK + t, blocks // 2, stride=2 * TOK), :] = plane
    for block in range(blocks):
        lanes = pl.ds(block * 128, 128)
        conv = tile[0, pl.ds(block * TOK, TOK), :]
        corr = tile[1, pl.ds(block * TOK, TOK), :]
        gq_ref[:, lanes] = (g_ref[:, lanes].astype(F32) * conv).astype(BF16)
        gk_ref[:, lanes] = (corr * v_ref[:, lanes].astype(F32)).astype(BF16)
        gv_ref[:, lanes] = (corr * k_ref[:, lanes].astype(F32)).astype(BF16)
    order = phase_order(gh_ref.shape[1], True)
    total = None
    for n in range(2):
        rows = [wide[pl.ds(2 * NPLANE + 2 * n + n2, NZ, stride=ZROWS), :] for n2 in range(2)]
        part = jnp.dot(jnp.concatenate(rows, axis=1).astype(BF16), order, preferred_element_type=F32)
        total = part if total is None else total + part
    gh_ref[...] = total


def columns(x):
    return jnp.concatenate([x[b : b + 128].T for b in range(0, x.shape[0], 128)], axis=1)


def row_pieces():
    for x in range(NX):
        for zh in range(NZH):
            for core in range(NCORE):
                for y in range(NY):
                    q = (((x * NZH + zh) * NCORE + core) * NZL) * NY + y
                    sent = ((x * NCORE + core) * NY + y) * PROWS + 2 * NZL * zh
                    yield q, sent


def read_taps(y, wide):
    shape = (TOK, 128)
    row, seg = row_of(shape), lane_of(shape) // 32
    out = []
    for x in range(NX):
        column = jnp.zeros(shape, F32)
        for core in range(NCORE):
            at = pl.multiple_of(((x * NCORE + core) * NY + y) * PROWS + 2 * NZ, 8)
            got = wide[pl.ds(at, 8), :]
            for zh in range(NZH):
                low, high = (got[4 * zh + n : 4 * zh + n + 1] + got[4 * zh + n + 2 : 4 * zh + n + 3] for n in range(2))
                both = jnp.where(row < 4, low, high)
                place = zh * NCORE + core
                for d in range(4):
                    moved = pltpu.roll(both, 32 * ((place - d) % 4), 1) if place != d else both
                    column = jnp.where((seg == place) & (row % 4 == d), moved, column)
        out.append(column)
    return jnp.concatenate(out, axis=1)


def write_lags(lags, wide):
    shape = (TOK, 128)
    row, seg = row_of(shape), lane_of(shape) // 32
    for x in range(NX):
        column = lags[:, x * 128 : x * 128 + 128]
        for core in range(NCORE):
            rows = []
            for zh in range(NZH):
                place = zh * NCORE + core
                spread = jnp.zeros(shape, F32)
                for d in range(4):
                    moved = pltpu.roll(column, 32 * ((d - place) % 4), 1) if place != d else column
                    spread = jnp.where((seg == d) & (row % 4 == d), moved, spread)
                pair = [jnp.sum(spread[4 * n : 4 * n + 4], axis=0, keepdims=True) for n in range(2)]
                high = [value.astype(BF16).astype(F32) for value in pair]
                rows += high + [value - h for value, h in zip(pair, high)]
            block = jnp.concatenate(rows, axis=0)
            for y in range(NY):
                wide[pl.ds(((x * NCORE + core) * NY + y) * PROWS + 2 * NZ, 8), :] = block


def group_kernel(r_ref, o_ref, wide, rows, lhs, ahead, hi, lo, flipped):
    count = rows.shape[1]
    nblk = count // ROWS
    lane8, row8 = lane_of((TOK, count)), row_of((TOK, count))
    wide[...] = r_ref[...].astype(F32)
    taps = read_taps(lax.axis_index("y"), wide)
    for p in range(TOK):
        skew = jnp.broadcast_to(taps[p : p + 1], (TOK, count))
        for bit in range(3):
            skew = jnp.where((row8 >> bit) & 1 == 1, pltpu.roll(skew, 1 << bit, 1), skew)
        for r in range(0, ROWS // 8, 2):
            pair = [
                jnp.where(lane8 >= row8 + 8 * n, pltpu.roll(skew, 8 * n, 1) if n else skew, 0.0) for n in (r, r + 1)
            ]
            high, low = halves(jnp.concatenate(pair, axis=0))
            hi[pl.ds(p * ROWS + 8 * r, 16), :], lo[pl.ds(p * ROWS + 8 * r, 16), :] = high, low
            flipped[pl.ds(8 * r, 16), pl.ds(p * count, count)] = high
            flipped[pl.ds(ROWS + 8 * r, 16), pl.ds(p * count, count)] = low
    for q, sent in row_pieces():
        for a in range(2):
            rows[a, pl.ds(q, NZL, stride=NY), :] = wide[pl.ds(sent + a, NZL, stride=2), :]
    sig, ups = rows[0], rows[1]
    sig_t, ups_t = columns(sig), columns(ups)
    lane = lane_of(sig_t.shape)
    sig_prev = jnp.where(lane == 0, 0.0, pltpu.roll(sig_t, 1, 1)).astype(BF16)
    ups_next = jnp.where(lane == count - 1, 0.0, pltpu.roll(ups_t, count - 1, 1)).astype(BF16)
    sig_t, ups_t = sig_t.astype(BF16), ups_t.astype(BF16)
    for p in range(TOK):
        cut = CH * p
        for b in range(nblk):
            cols = slice(b * 128, b * 128 + 128)
            if p:
                lhs[pl.ds(b * 128, cut), pl.ds(p * 128, 128)] = sig_prev[128 - cut :, cols]
            lhs[pl.ds(b * 128 + cut, 128 - cut), pl.ds(p * 128, 128)] = sig_t[: 128 - cut, cols]
            size = count - 128 * b
            ahead[pl.ds(b * 128, 128 - cut), pl.ds(p * count, size)] = ups_t[cut:, b * 128 :]
            if p:
                ahead[pl.ds(b * 128 + 128 - cut, cut), pl.ds(p * count, size)] = ups_next[:cut, b * 128 :]
            if b:
                ahead[pl.ds(b * 128, 128), pl.ds(p * count + size, 128 * b)] = jnp.zeros((128, 128 * b), BF16)
    side = jnp.concatenate([sig[b * 128 : b * 128 + 128] for b in range(nblk)], axis=1).astype(BF16)
    sums = []
    for p in range(TOK):
        lags = jnp.dot(side, ahead[:, pl.ds(p * count, count)], preferred_element_type=F32)
        total = jnp.zeros((TOK, count), F32)
        for r in range(ROWS // 8):
            part = jnp.where(lane8 >= row8 + 8 * r, lags[8 * r : 8 * r + 8], 0.0)
            total = total + (pltpu.roll(part, count - 8 * r, 1) if r else part)
        for bit in range(3):
            total = jnp.where((row8 >> bit) & 1 == 1, pltpu.roll(total, count - (1 << bit), 1), total)
        sums.append(jnp.sum(total, axis=0, keepdims=True))
    write_lags(jnp.concatenate(sums, axis=0), wide)
    conv = [None] * nblk
    for b in range(nblk):
        block = lhs[pl.ds(b * 128, 128), :]
        size = count - 128 * b
        part = jnp.dot(block, hi[:, pl.ds(0, size)], preferred_element_type=F32)
        part = part + jnp.dot(block, lo[:, pl.ds(0, size)], preferred_element_type=F32)
        for k in range(nblk - b):
            piece = part[:, k * 128 : k * 128 + 128]
            conv[b + k] = piece if conv[b + k] is None else conv[b + k] + piece
    back = lax.dot_general(ahead[...], flipped[...], (((1,), (1,)), ((), ())), preferred_element_type=F32)
    for b in range(nblk):
        at = pl.ds(b * 128, 128)
        rows[0, at, :] = conv[b].T
        rows[1, at, :] = (back[b * 128 : b * 128 + 128, :128] + back[b * 128 : b * 128 + 128, 128:]).T
    for q, sent in row_pieces():
        for a in range(2):
            wide[pl.ds(sent + a, NZL, stride=2), :] = rows[a, pl.ds(q, NZL, stride=NY), :]
    o_ref[...] = wide[...].astype(BF16)


def params(mib):
    return pltpu.CompilerParams(vmem_limit_bytes=mib << 20)


def pack(query, key, value, grad, filters):
    rows = query.shape[1] // CH
    return pl.pallas_call(
        pack_kernel,
        out_shape=jax.ShapeDtypeStruct((NZ * ZROWS, 128), BF16),
        in_specs=[pl.BlockSpec(memory_space=pltpu.HBM)] * 5,
        scratch_shapes=[
            pltpu.VMEM((4, *query.shape), BF16),
            pltpu.VMEM(filters.shape, F32),
            pltpu.VMEM((2, rows, 128), F32),
            pltpu.VMEM((NZ * ZROWS, 128), F32),
            pltpu.SemaphoreType.DMA((5,)),
        ],
        compiler_params=params(8),
        name="pack",
    )(*(pltpu.with_memory_space_constraint(x, pltpu.HBM) for x in (key, value, grad, query, filters)))


def unpack(received, key, value, grad, filters):
    shape = jax.ShapeDtypeStruct(key.shape, BF16)
    rows = key.shape[1] // CH
    return pl.pallas_call(
        unpack_kernel,
        out_shape=(shape, shape, shape, jax.ShapeDtypeStruct(filters.shape, F32)),
        scratch_shapes=[pltpu.VMEM((2, rows, 128), F32), pltpu.VMEM((NZ * ZROWS, 128), F32)],
        compiler_params=params(8),
        name="unpack",
    )(received, key, value, grad)


def inward(received):
    return pl.pallas_call(
        inward_kernel,
        out_shape=jax.ShapeDtypeStruct((NPLANE * PROWS, 128), BF16),
        scratch_shapes=[pltpu.VMEM((NZ * ZROWS, 128), F32), pltpu.VMEM((NPLANE * PROWS, 128), F32)],
        compiler_params=params(8),
        name="inward",
    )(received)


def outward(received):
    return pl.pallas_call(
        outward_kernel,
        out_shape=jax.ShapeDtypeStruct((NZ * ZROWS, 128), BF16),
        scratch_shapes=[pltpu.VMEM((NPLANE * PROWS, 128), F32), pltpu.VMEM((NZ * ZROWS, 128), F32)],
        compiler_params=params(8),
        name="outward",
    )(received)


def group(received):
    count = NZ * NPLANE
    return pl.pallas_call(
        group_kernel,
        out_shape=jax.ShapeDtypeStruct(received.shape, BF16),
        scratch_shapes=[
            pltpu.VMEM(received.shape, F32),
            pltpu.VMEM((2, count, 128), F32),
            pltpu.VMEM((count, TOK * ROWS), BF16),
            pltpu.VMEM((count, TOK * count), BF16),
            pltpu.VMEM((TOK * ROWS, count), BF16),
            pltpu.VMEM((TOK * ROWS, count), BF16),
            pltpu.VMEM((2 * ROWS, TOK * count), BF16),
        ],
        compiler_params=params(32),
        name="group",
    )(received)


def exchange(rows, axes):
    chunks = rows.reshape(-1, 4, 128)
    return lax.all_to_all(chunks, axes, 0, 0, tiled=True).reshape(rows.shape)


def on_device(query_gate, key_gate, value_proj, grad_out, long_filters):
    rows = pack(query_gate, key_gate, value_proj, grad_out, long_filters)
    rows = inward(exchange(rows, Z_AXES))
    rows = group(exchange(rows, PLANE_AXES))
    rows = outward(exchange(rows, PLANE_AXES))
    return unpack(exchange(rows, Z_AXES), key_gate, value_proj, grad_out, long_filters)


def solution(mesh):
    fine = Mesh(mesh.devices.reshape(NX, NZH, NCORE, NZL, NY), ("x", "zh", "core", "zl", "y"))
    tokens = P(("x", "zh", "core", "zl", "y"), None)
    filters = P(("zl", "y"), ("x", "zh", "core"))
    return jax.shard_map(
        on_device,
        mesh=fine,
        in_specs=(tokens, tokens, tokens, tokens, filters),
        out_specs=(tokens, tokens, tokens, filters),
        check_vma=False,
    )
```

```python
import jax
import jax.numpy as jnp
from jax import lax
from jax.experimental import pallas as pl
from jax.experimental.pallas import tpu as pltpu
from jax.sharding import Mesh
from jax.sharding import PartitionSpec as P

CH = 16
TOK = 8
ROWS = 128
NX, NZH, NCORE, NZL, NY = 4, 2, 2, 8, 4
NZ = NZH * NZL
NPLANE = NX * NCORE * NY
ZROWS = 2 * NPLANE + 4
PROWS = 2 * NZ + 8
Z_AXES = ("zh", "zl")
PLANE_AXES = ("x", "core", "y")
F32 = jnp.float32
BF16 = jnp.bfloat16


def lane_of(shape):
    return lax.broadcasted_iota(jnp.int32, shape, 1)


def row_of(shape):
    return lax.broadcasted_iota(jnp.int32, shape, 0)


def swap_segments(planes):
    planes = list(planes)
    seg = lane_of(planes[0].shape) // CH
    for bit in range(3):
        step = 1 << bit
        odd = (seg >> bit) & 1 == 1
        for low in range(TOK):
            if low & step:
                continue
            first, second = planes[low], planes[low + step]
            planes[low] = jnp.where(odd, pltpu.roll(second, CH * step, 1), first)
            planes[low + step] = jnp.where(odd, second, pltpu.roll(first, 128 - CH * step, 1))
    return planes


def phase_order(taps, back):
    shape = (taps, taps)
    source, target = row_of(shape), lane_of(shape)
    if back:
        source, target = target, source
    fine = taps // TOK
    return jnp.where((source % TOK) * fine + source // TOK == target, 1.0, 0.0).astype(BF16)


def halves(x):
    high = x.astype(BF16)
    return high, (x - high.astype(F32)).astype(BF16)


def pack_kernel(k_hbm, v_hbm, g_hbm, q_hbm, h_hbm, o_ref, inputs, taps, tile, wide, sems):
    copies = [
        pltpu.make_async_copy(hbm, inputs.at[n], sems.at[n]) for n, hbm in enumerate((k_hbm, v_hbm, g_hbm, q_hbm))
    ]
    copies.append(pltpu.make_async_copy(h_hbm, taps, sems.at[4]))
    for copy in copies[4:] + copies[:4]:
        copy.start()
    order = phase_order(taps.shape[1], False)
    copies[4].wait()
    for n, part in enumerate(halves(taps[...])):
        part = jnp.dot(part, order, preferred_element_type=F32)
        for n2 in range(2):
            wide[pl.ds(2 * NPLANE + 2 * n + n2, NZ, stride=ZROWS), :] = part[:, 128 * n2 : 128 * n2 + 128]
    blocks = k_hbm.shape[1] // 128
    for a in range(2):
        copies[2 * a].wait()
        copies[2 * a + 1].wait()
        for block in range(blocks):
            lanes = pl.ds(block * 128, 128)
            prod = (inputs[2 * a, :, lanes].astype(F32) * inputs[2 * a + 1, :, lanes].astype(F32)).astype(BF16)
            tile[a, pl.ds(block * TOK, TOK), :] = prod.astype(F32)
        for half in range(2):
            planes = [tile[a, pl.ds(half * TOK + t, blocks // 2, stride=2 * TOK), :] for t in range(TOK)]
            for i, plane in enumerate(swap_segments(planes)):
                wide[pl.ds((half * TOK + i) * ZROWS + a, blocks // 2, stride=2), :] = plane
    o_ref[...] = wide[...].astype(BF16)


def inward_kernel(r_ref, o_ref, before, after):
    before[...] = r_ref[...].astype(F32)
    for j in range(NPLANE):
        for a in range(2):
            after[pl.ds(PROWS * j + a, NZ, stride=2), :] = before[pl.ds(2 * j + a, NZ, stride=ZROWS), :]
    for zl in range(NZL):
        parts = [before[pl.ds((zh * NZL + zl) * ZROWS + 2 * NPLANE, 4), :] for zh in range(NZH)]
        block = jnp.concatenate(parts, axis=0)
        for y in range(NY):
            after[pl.ds((zl * NY + y) * PROWS + 2 * NZ, 8), :] = block
    o_ref[...] = after[...].astype(BF16)


def outward_kernel(r_ref, o_ref, before, after):
    own = lax.axis_index("y")
    before[...] = r_ref[...].astype(F32)
    for j in range(NPLANE):
        for a in range(2):
            after[pl.ds(2 * j + a, NZ, stride=ZROWS), :] = before[pl.ds(PROWS * j + a, NZ, stride=2), :]
    for zl in range(NZL):
        at = pl.multiple_of((zl * NY + own) * PROWS + 2 * NZ, 8)
        block = before[pl.ds(at, 8), :]
        for zh in range(NZH):
            after[pl.ds((zh * NZL + zl) * ZROWS + 2 * NPLANE, 4), :] = block[4 * zh : 4 * zh + 4]
    o_ref[...] = after[...].astype(BF16)


def unpack_kernel(r_ref, k_ref, v_ref, g_ref, gq_ref, gk_ref, gv_ref, gh_ref, tile, wide):
    blocks = k_ref.shape[1] // 128
    wide[...] = r_ref[...].astype(F32)
    for a in range(2):
        for half in range(2):
            planes = [
                wide[pl.ds((half * TOK + i) * ZROWS + a, blocks // 2, stride=2), :] for i in range(TOK)
            ]
            for t, plane in enumerate(swap_segments(planes)):
                tile[a, pl.ds(half * TOK + t, blocks // 2, stride=2 * TOK), :] = plane
    for block in range(blocks):
        lanes = pl.ds(block * 128, 128)
        conv = tile[0, pl.ds(block * TOK, TOK), :]
        corr = tile[1, pl.ds(block * TOK, TOK), :]
        gq_ref[:, lanes] = (g_ref[:, lanes].astype(F32) * conv).astype(BF16)
        gk_ref[:, lanes] = (corr * v_ref[:, lanes].astype(F32)).astype(BF16)
        gv_ref[:, lanes] = (corr * k_ref[:, lanes].astype(F32)).astype(BF16)
    order = phase_order(gh_ref.shape[1], True)
    total = None
    for n in range(2):
        rows = [wide[pl.ds(2 * NPLANE + 2 * n + n2, NZ, stride=ZROWS), :] for n2 in range(2)]
        part = jnp.dot(jnp.concatenate(rows, axis=1).astype(BF16), order, preferred_element_type=F32)
        total = part if total is None else total + part
    gh_ref[...] = total


def columns(x):
    return jnp.concatenate([x[b : b + 128].T for b in range(0, x.shape[0], 128)], axis=1)


def row_pieces():
    for x in range(NX):
        for zh in range(NZH):
            for core in range(NCORE):
                for y in range(NY):
                    q = (((x * NZH + zh) * NCORE + core) * NZL) * NY + y
                    sent = ((x * NCORE + core) * NY + y) * PROWS + 2 * NZL * zh
                    yield q, sent


def read_taps(y, wide):
    shape = (TOK, 128)
    row, seg = row_of(shape), lane_of(shape) // 32
    out = []
    for x in range(NX):
        column = jnp.zeros(shape, F32)
        for core in range(NCORE):
            at = pl.multiple_of(((x * NCORE + core) * NY + y) * PROWS + 2 * NZ, 8)
            got = wide[pl.ds(at, 8), :]
            for zh in range(NZH):
                low, high = (got[4 * zh + n : 4 * zh + n + 1] + got[4 * zh + n + 2 : 4 * zh + n + 3] for n in range(2))
                both = jnp.where(row < 4, low, high)
                place = zh * NCORE + core
                for d in range(4):
                    moved = pltpu.roll(both, 32 * ((place - d) % 4), 1) if place != d else both
                    column = jnp.where((seg == place) & (row % 4 == d), moved, column)
        out.append(column)
    return jnp.concatenate(out, axis=1)


def write_lags(lags, wide):
    shape = (TOK, 128)
    row, seg = row_of(shape), lane_of(shape) // 32
    for x in range(NX):
        column = lags[:, x * 128 : x * 128 + 128]
        for core in range(NCORE):
            rows = []
            for zh in range(NZH):
                place = zh * NCORE + core
                spread = jnp.zeros(shape, F32)
                for d in range(4):
                    moved = pltpu.roll(column, 32 * ((d - place) % 4), 1) if place != d else column
                    spread = jnp.where((seg == d) & (row % 4 == d), moved, spread)
                pair = [jnp.sum(spread[4 * n : 4 * n + 4], axis=0, keepdims=True) for n in range(2)]
                high = [value.astype(BF16).astype(F32) for value in pair]
                rows += high + [value - h for value, h in zip(pair, high)]
            block = jnp.concatenate(rows, axis=0)
            for y in range(NY):
                wide[pl.ds(((x * NCORE + core) * NY + y) * PROWS + 2 * NZ, 8), :] = block


def group_kernel(r_ref, o_ref, wide, rows, lhs, ahead, hi, lo, flipped):
    count = rows.shape[1]
    nblk = count // ROWS
    lane8, row8 = lane_of((TOK, count)), row_of((TOK, count))
    wide[...] = r_ref[...].astype(F32)
    taps = read_taps(lax.axis_index("y"), wide)
    for p in range(TOK):
        skew = jnp.broadcast_to(taps[p : p + 1], (TOK, count))
        for bit in range(3):
            skew = jnp.where((row8 >> bit) & 1 == 1, pltpu.roll(skew, 1 << bit, 1), skew)
        for r in range(0, ROWS // 8, 2):
            pair = [
                jnp.where(lane8 >= row8 + 8 * n, pltpu.roll(skew, 8 * n, 1) if n else skew, 0.0) for n in (r, r + 1)
            ]
            high, low = halves(jnp.concatenate(pair, axis=0))
            hi[pl.ds(p * ROWS + 8 * r, 16), :], lo[pl.ds(p * ROWS + 8 * r, 16), :] = high, low
            flipped[pl.ds(8 * r, 16), pl.ds(p * count, count)] = high
            flipped[pl.ds(ROWS + 8 * r, 16), pl.ds(p * count, count)] = low
    for q, sent in row_pieces():
        for a in range(2):
            rows[a, pl.ds(q, NZL, stride=NY), :] = wide[pl.ds(sent + a, NZL, stride=2), :]
    sig, ups = rows[0], rows[1]
    sig_t, ups_t = columns(sig), columns(ups)
    lane = lane_of(sig_t.shape)
    sig_prev = jnp.where(lane == 0, 0.0, pltpu.roll(sig_t, 1, 1)).astype(BF16)
    ups_next = jnp.where(lane == count - 1, 0.0, pltpu.roll(ups_t, count - 1, 1)).astype(BF16)
    sig_t, ups_t = sig_t.astype(BF16), ups_t.astype(BF16)
    for p in range(TOK):
        cut = CH * p
        for b in range(nblk):
            cols = slice(b * 128, b * 128 + 128)
            if p:
                lhs[pl.ds(b * 128, cut), pl.ds(p * 128, 128)] = sig_prev[128 - cut :, cols]
            lhs[pl.ds(b * 128 + cut, 128 - cut), pl.ds(p * 128, 128)] = sig_t[: 128 - cut, cols]
            size = count - 128 * b
            ahead[pl.ds(b * 128, 128 - cut), pl.ds(p * count, size)] = ups_t[cut:, b * 128 :]
            if p:
                ahead[pl.ds(b * 128 + 128 - cut, cut), pl.ds(p * count, size)] = ups_next[:cut, b * 128 :]
            if b:
                ahead[pl.ds(b * 128, 128), pl.ds(p * count + size, 128 * b)] = jnp.zeros((128, 128 * b), BF16)
    side = jnp.concatenate([sig[b * 128 : b * 128 + 128] for b in range(nblk)], axis=1).astype(BF16)
    sums = []
    for p in range(TOK):
        lags = jnp.dot(side, ahead[:, pl.ds(p * count, count)], preferred_element_type=F32)
        total = jnp.zeros((TOK, count), F32)
        for r in range(ROWS // 8):
            part = jnp.where(lane8 >= row8 + 8 * r, lags[8 * r : 8 * r + 8], 0.0)
            total = total + (pltpu.roll(part, count - 8 * r, 1) if r else part)
        for bit in range(3):
            total = jnp.where((row8 >> bit) & 1 == 1, pltpu.roll(total, count - (1 << bit), 1), total)
        sums.append(jnp.sum(total, axis=0, keepdims=True))
    write_lags(jnp.concatenate(sums, axis=0), wide)
    conv = [None] * nblk
    for b in range(nblk):
        block = lhs[pl.ds(b * 128, 128), :]
        size = count - 128 * b
        part = jnp.dot(block, hi[:, pl.ds(0, size)], preferred_element_type=F32)
        part = part + jnp.dot(block, lo[:, pl.ds(0, size)], preferred_element_type=F32)
        for k in range(nblk - b):
            piece = part[:, k * 128 : k * 128 + 128]
            conv[b + k] = piece if conv[b + k] is None else conv[b + k] + piece
    back = lax.dot_general(flipped[...], ahead[...], (((1,), (1,)), ((), ())), preferred_element_type=F32)
    for b in range(nblk):
        at = pl.ds(b * 128, 128)
        rows[0, at, :] = conv[b].T
        rows[1, at, :] = back[:128, b * 128 : b * 128 + 128] + back[128:, b * 128 : b * 128 + 128]
    for q, sent in row_pieces():
        for a in range(2):
            wide[pl.ds(sent + a, NZL, stride=2), :] = rows[a, pl.ds(q, NZL, stride=NY), :]
    o_ref[...] = wide[...].astype(BF16)


def params(mib):
    return pltpu.CompilerParams(vmem_limit_bytes=mib << 20)


def pack(query, key, value, grad, filters):
    rows = query.shape[1] // CH
    return pl.pallas_call(
        pack_kernel,
        out_shape=jax.ShapeDtypeStruct((NZ * ZROWS, 128), BF16),
        in_specs=[pl.BlockSpec(memory_space=pltpu.HBM)] * 5,
        scratch_shapes=[
            pltpu.VMEM((4, *query.shape), BF16),
            pltpu.VMEM(filters.shape, F32),
            pltpu.VMEM((2, rows, 128), F32),
            pltpu.VMEM((NZ * ZROWS, 128), F32),
            pltpu.SemaphoreType.DMA((5,)),
        ],
        compiler_params=params(8),
        name="pack",
    )(*(pltpu.with_memory_space_constraint(x, pltpu.HBM) for x in (key, value, grad, query, filters)))


def unpack(received, key, value, grad, filters):
    shape = jax.ShapeDtypeStruct(key.shape, BF16)
    rows = key.shape[1] // CH
    return pl.pallas_call(
        unpack_kernel,
        out_shape=(shape, shape, shape, jax.ShapeDtypeStruct(filters.shape, F32)),
        scratch_shapes=[pltpu.VMEM((2, rows, 128), F32), pltpu.VMEM((NZ * ZROWS, 128), F32)],
        compiler_params=params(8),
        name="unpack",
    )(received, key, value, grad)


def inward(received):
    return pl.pallas_call(
        inward_kernel,
        out_shape=jax.ShapeDtypeStruct((NPLANE * PROWS, 128), BF16),
        scratch_shapes=[pltpu.VMEM((NZ * ZROWS, 128), F32), pltpu.VMEM((NPLANE * PROWS, 128), F32)],
        compiler_params=params(8),
        name="inward",
    )(received)


def outward(received):
    return pl.pallas_call(
        outward_kernel,
        out_shape=jax.ShapeDtypeStruct((NZ * ZROWS, 128), BF16),
        scratch_shapes=[pltpu.VMEM((NPLANE * PROWS, 128), F32), pltpu.VMEM((NZ * ZROWS, 128), F32)],
        compiler_params=params(8),
        name="outward",
    )(received)


def group(received):
    count = NZ * NPLANE
    return pl.pallas_call(
        group_kernel,
        out_shape=jax.ShapeDtypeStruct(received.shape, BF16),
        scratch_shapes=[
            pltpu.VMEM(received.shape, F32),
            pltpu.VMEM((2, count, 128), F32),
            pltpu.VMEM((count, TOK * ROWS), BF16),
            pltpu.VMEM((count, TOK * count), BF16),
            pltpu.VMEM((TOK * ROWS, count), BF16),
            pltpu.VMEM((TOK * ROWS, count), BF16),
            pltpu.VMEM((2 * ROWS, TOK * count), BF16),
        ],
        compiler_params=params(32),
        name="group",
    )(received)


def exchange(rows, axes):
    chunks = rows.reshape(-1, 4, 128)
    return lax.all_to_all(chunks, axes, 0, 0, tiled=True).reshape(rows.shape)


def on_device(query_gate, key_gate, value_proj, grad_out, long_filters):
    rows = pack(query_gate, key_gate, value_proj, grad_out, long_filters)
    rows = inward(exchange(rows, Z_AXES))
    rows = group(exchange(rows, PLANE_AXES))
    rows = outward(exchange(rows, PLANE_AXES))
    return unpack(exchange(rows, Z_AXES), key_gate, value_proj, grad_out, long_filters)


def solution(mesh):
    fine = Mesh(mesh.devices.reshape(NX, NZH, NCORE, NZL, NY), ("x", "zh", "core", "zl", "y"))
    tokens = P(("x", "zh", "core", "zl", "y"), None)
    filters = P(("zl", "y"), ("x", "zh", "core"))
    return jax.shard_map(
        on_device,
        mesh=fine,
        in_specs=(tokens, tokens, tokens, tokens, filters),
        out_specs=(tokens, tokens, tokens, filters),
        check_vma=False,
    )
```

```python
import jax
import jax.numpy as jnp
from jax import lax
from jax.experimental import pallas as pl
from jax.experimental.pallas import tpu as pltpu
from jax.sharding import Mesh
from jax.sharding import PartitionSpec as P

CH = 16
TOK = 8
ROWS = 128
NX, NZH, NCORE, NZL, NY = 4, 2, 2, 8, 4
NZ = NZH * NZL
NPLANE = NX * NCORE * NY
ZROWS = 2 * NPLANE + 4
PROWS = 2 * NZ + 8
ZBACK = 2 * NPLANE + 2
PBACK = 2 * NZ + 4
Z_AXES = ("zh", "zl")
PLANE_AXES = ("x", "core", "y")
F32 = jnp.float32
BF16 = jnp.bfloat16


def lane_of(shape):
    return lax.broadcasted_iota(jnp.int32, shape, 1)


def row_of(shape):
    return lax.broadcasted_iota(jnp.int32, shape, 0)


def swap_segments(planes):
    planes = list(planes)
    seg = lane_of(planes[0].shape) // CH
    for bit in range(3):
        step = 1 << bit
        odd = (seg >> bit) & 1 == 1
        for low in range(TOK):
            if low & step:
                continue
            first, second = planes[low], planes[low + step]
            planes[low] = jnp.where(odd, pltpu.roll(second, CH * step, 1), first)
            planes[low + step] = jnp.where(odd, second, pltpu.roll(first, 128 - CH * step, 1))
    return planes


def phase_order(taps, back):
    shape = (taps, taps)
    source, target = row_of(shape), lane_of(shape)
    if back:
        source, target = target, source
    fine = taps // TOK
    return jnp.where((source % TOK) * fine + source // TOK == target, 1.0, 0.0).astype(BF16)


def halves(x):
    high = x.astype(BF16)
    return high, (x - high.astype(F32)).astype(BF16)


def pack_kernel(k_hbm, v_hbm, g_hbm, q_hbm, h_hbm, o_ref, inputs, taps, tile, wide, sems):
    copies = [
        pltpu.make_async_copy(hbm, inputs.at[n], sems.at[n]) for n, hbm in enumerate((k_hbm, v_hbm, g_hbm, q_hbm))
    ]
    copies.append(pltpu.make_async_copy(h_hbm, taps, sems.at[4]))
    for copy in copies[4:] + copies[:4]:
        copy.start()
    order = phase_order(taps.shape[1], False)
    copies[4].wait()
    for n, part in enumerate(halves(taps[...])):
        part = jnp.dot(part, order, preferred_element_type=F32)
        for n2 in range(2):
            wide[pl.ds(2 * NPLANE + 2 * n + n2, NZ, stride=ZROWS), :] = part[:, 128 * n2 : 128 * n2 + 128]
    blocks = k_hbm.shape[1] // 128
    for a in range(2):
        copies[2 * a].wait()
        copies[2 * a + 1].wait()
        for block in range(blocks):
            lanes = pl.ds(block * 128, 128)
            prod = (inputs[2 * a, :, lanes].astype(F32) * inputs[2 * a + 1, :, lanes].astype(F32)).astype(BF16)
            tile[a, pl.ds(block * TOK, TOK), :] = prod.astype(F32)
        for half in range(2):
            planes = [tile[a, pl.ds(half * TOK + t, blocks // 2, stride=2 * TOK), :] for t in range(TOK)]
            for i, plane in enumerate(swap_segments(planes)):
                wide[pl.ds((half * TOK + i) * ZROWS + a, blocks // 2, stride=2), :] = plane
    o_ref[...] = wide[...].astype(BF16)


def inward_kernel(r_ref, o_ref, before, after):
    before[...] = r_ref[...].astype(F32)
    for j in range(NPLANE):
        for a in range(2):
            after[pl.ds(PROWS * j + a, NZ, stride=2), :] = before[pl.ds(2 * j + a, NZ, stride=ZROWS), :]
    for zl in range(NZL):
        parts = [before[pl.ds((zh * NZL + zl) * ZROWS + 2 * NPLANE, 4), :] for zh in range(NZH)]
        block = jnp.concatenate(parts, axis=0)
        for y in range(NY):
            after[pl.ds((zl * NY + y) * PROWS + 2 * NZ, 8), :] = block
    o_ref[...] = after[...].astype(BF16)


def outward_kernel(r_ref, o_ref, before, after):
    own = lax.axis_index("y")
    before[...] = r_ref[...].astype(F32)
    for j in range(NPLANE):
        for a in range(2):
            after[pl.ds(2 * j + a, NZ, stride=ZBACK), :] = before[pl.ds(PBACK * j + a, NZ, stride=2), :]
    for zl in range(NZL):
        at = pl.multiple_of((zl * NY + own) * PBACK + 2 * NZ, 4)
        block = before[pl.ds(at, 4), :]
        for zh in range(NZH):
            after[pl.ds((zh * NZL + zl) * ZBACK + 2 * NPLANE, 2), :] = block[2 * zh : 2 * zh + 2]
    o_ref[...] = after[...].astype(BF16)


def unpack_kernel(r_ref, k_ref, v_ref, g_ref, gq_ref, gk_ref, gv_ref, gh_ref, tile, wide):
    blocks = k_ref.shape[1] // 128
    wide[...] = r_ref[...].astype(F32)
    for a in range(2):
        for half in range(2):
            planes = [
                wide[pl.ds((half * TOK + i) * ZBACK + a, blocks // 2, stride=2), :] for i in range(TOK)
            ]
            for t, plane in enumerate(swap_segments(planes)):
                tile[a, pl.ds(half * TOK + t, blocks // 2, stride=2 * TOK), :] = plane
    for block in range(blocks):
        lanes = pl.ds(block * 128, 128)
        conv = tile[0, pl.ds(block * TOK, TOK), :]
        corr = tile[1, pl.ds(block * TOK, TOK), :]
        gq_ref[:, lanes] = (g_ref[:, lanes].astype(F32) * conv).astype(BF16)
        gk_ref[:, lanes] = (corr * v_ref[:, lanes].astype(F32)).astype(BF16)
        gv_ref[:, lanes] = (corr * k_ref[:, lanes].astype(F32)).astype(BF16)
    order = phase_order(gh_ref.shape[1], True)
    rows = [wide[pl.ds(2 * NPLANE + n, NZ, stride=ZBACK), :] for n in range(2)]
    gh_ref[...] = jnp.dot(jnp.concatenate(rows, axis=1).astype(BF16), order, preferred_element_type=F32)


def columns(x):
    return jnp.concatenate([x[b : b + 128].T for b in range(0, x.shape[0], 128)], axis=1)


def row_pieces(stride):
    for x in range(NX):
        for zh in range(NZH):
            for core in range(NCORE):
                for y in range(NY):
                    q = (((x * NZH + zh) * NCORE + core) * NZL) * NY + y
                    sent = ((x * NCORE + core) * NY + y) * stride + 2 * NZL * zh
                    yield q, sent


def read_taps(y, wide):
    shape = (TOK, 128)
    row, seg = row_of(shape), lane_of(shape) // 32
    out = []
    for x in range(NX):
        column = jnp.zeros(shape, F32)
        for core in range(NCORE):
            at = pl.multiple_of(((x * NCORE + core) * NY + y) * PROWS + 2 * NZ, 8)
            got = wide[pl.ds(at, 8), :]
            for zh in range(NZH):
                low, high = (got[4 * zh + n : 4 * zh + n + 1] + got[4 * zh + n + 2 : 4 * zh + n + 3] for n in range(2))
                both = jnp.where(row < 4, low, high)
                place = zh * NCORE + core
                for d in range(4):
                    moved = pltpu.roll(both, 32 * ((place - d) % 4), 1) if place != d else both
                    column = jnp.where((seg == place) & (row % 4 == d), moved, column)
        out.append(column)
    return jnp.concatenate(out, axis=1)


def write_lags(lags, wide):
    shape = (TOK, 128)
    row, seg = row_of(shape), lane_of(shape) // 32
    for x in range(NX):
        column = lags[:, x * 128 : x * 128 + 128]
        for core in range(NCORE):
            rows = []
            for zh in range(NZH):
                place = zh * NCORE + core
                spread = jnp.zeros(shape, F32)
                for d in range(4):
                    moved = pltpu.roll(column, 32 * ((d - place) % 4), 1) if place != d else column
                    spread = jnp.where((seg == d) & (row % 4 == d), moved, spread)
                rows += [jnp.sum(spread[4 * n : 4 * n + 4], axis=0, keepdims=True) for n in range(2)]
            block = jnp.concatenate(rows, axis=0)
            for y in range(NY):
                wide[pl.ds(((x * NCORE + core) * NY + y) * PBACK + 2 * NZ, 4), :] = block


def group_kernel(r_ref, o_ref, wide, rows, lhs, ahead, hi, lo, flipped):
    count = rows.shape[1]
    nblk = count // ROWS
    lane8, row8 = lane_of((TOK, count)), row_of((TOK, count))
    wide[...] = r_ref[...].astype(F32)
    taps = read_taps(lax.axis_index("y"), wide)
    for p in range(TOK):
        skew = jnp.broadcast_to(taps[p : p + 1], (TOK, count))
        for bit in range(3):
            skew = jnp.where((row8 >> bit) & 1 == 1, pltpu.roll(skew, 1 << bit, 1), skew)
        for r in range(0, ROWS // 8, 2):
            pair = [
                jnp.where(lane8 >= row8 + 8 * n, pltpu.roll(skew, 8 * n, 1) if n else skew, 0.0) for n in (r, r + 1)
            ]
            high, low = halves(jnp.concatenate(pair, axis=0))
            hi[pl.ds(p * ROWS + 8 * r, 16), :], lo[pl.ds(p * ROWS + 8 * r, 16), :] = high, low
            flipped[pl.ds(8 * r, 16), pl.ds(p * count, count)] = high
            flipped[pl.ds(ROWS + 8 * r, 16), pl.ds(p * count, count)] = low
    for q, sent in row_pieces(PROWS):
        for a in range(2):
            rows[a, pl.ds(q, NZL, stride=NY), :] = wide[pl.ds(sent + a, NZL, stride=2), :]
    sig, ups = rows[0], rows[1]
    sig_t, ups_t = columns(sig), columns(ups)
    lane = lane_of(sig_t.shape)
    sig_prev = jnp.where(lane == 0, 0.0, pltpu.roll(sig_t, 1, 1)).astype(BF16)
    ups_next = jnp.where(lane == count - 1, 0.0, pltpu.roll(ups_t, count - 1, 1)).astype(BF16)
    sig_t, ups_t = sig_t.astype(BF16), ups_t.astype(BF16)
    for p in range(TOK):
        cut = CH * p
        for b in range(nblk):
            cols = slice(b * 128, b * 128 + 128)
            if p:
                lhs[pl.ds(b * 128, cut), pl.ds(p * 128, 128)] = sig_prev[128 - cut :, cols]
            lhs[pl.ds(b * 128 + cut, 128 - cut), pl.ds(p * 128, 128)] = sig_t[: 128 - cut, cols]
            size = count - 128 * b
            ahead[pl.ds(b * 128, 128 - cut), pl.ds(p * count, size)] = ups_t[cut:, b * 128 :]
            if p:
                ahead[pl.ds(b * 128 + 128 - cut, cut), pl.ds(p * count, size)] = ups_next[:cut, b * 128 :]
            if b:
                ahead[pl.ds(b * 128, 128), pl.ds(p * count + size, 128 * b)] = jnp.zeros((128, 128 * b), BF16)
    side = jnp.concatenate([sig[b * 128 : b * 128 + 128] for b in range(nblk)], axis=1).astype(BF16)
    sums = []
    for p in range(TOK):
        lags = jnp.dot(side, ahead[:, pl.ds(p * count, count)], preferred_element_type=F32)
        total = jnp.zeros((TOK, count), F32)
        for r in range(ROWS // 8):
            part = jnp.where(lane8 >= row8 + 8 * r, lags[8 * r : 8 * r + 8], 0.0)
            total = total + (pltpu.roll(part, count - 8 * r, 1) if r else part)
        for bit in range(3):
            total = jnp.where((row8 >> bit) & 1 == 1, pltpu.roll(total, count - (1 << bit), 1), total)
        sums.append(jnp.sum(total, axis=0, keepdims=True))
    write_lags(jnp.concatenate(sums, axis=0), wide)
    conv = [None] * nblk
    for b in range(nblk):
        block = lhs[pl.ds(b * 128, 128), :]
        size = count - 128 * b
        part = jnp.dot(block, hi[:, pl.ds(0, size)], preferred_element_type=F32)
        part = part + jnp.dot(block, lo[:, pl.ds(0, size)], preferred_element_type=F32)
        for k in range(nblk - b):
            piece = part[:, k * 128 : k * 128 + 128]
            conv[b + k] = piece if conv[b + k] is None else conv[b + k] + piece
    back = lax.dot_general(flipped[...], ahead[...], (((1,), (1,)), ((), ())), preferred_element_type=F32)
    for b in range(nblk):
        at = pl.ds(b * 128, 128)
        rows[0, at, :] = conv[b].T
        rows[1, at, :] = back[:128, b * 128 : b * 128 + 128] + back[128:, b * 128 : b * 128 + 128]
    for q, sent in row_pieces(PBACK):
        for a in range(2):
            wide[pl.ds(sent + a, NZL, stride=2), :] = rows[a, pl.ds(q, NZL, stride=NY), :]
    o_ref[...] = wide[pl.ds(0, NPLANE * PBACK), :].astype(BF16)


def params(mib):
    return pltpu.CompilerParams(vmem_limit_bytes=mib << 20)


def pack(query, key, value, grad, filters):
    rows = query.shape[1] // CH
    return pl.pallas_call(
        pack_kernel,
        out_shape=jax.ShapeDtypeStruct((NZ * ZROWS, 128), BF16),
        in_specs=[pl.BlockSpec(memory_space=pltpu.HBM)] * 5,
        scratch_shapes=[
            pltpu.VMEM((4, *query.shape), BF16),
            pltpu.VMEM(filters.shape, F32),
            pltpu.VMEM((2, rows, 128), F32),
            pltpu.VMEM((NZ * ZROWS, 128), F32),
            pltpu.SemaphoreType.DMA((5,)),
        ],
        compiler_params=params(8),
        name="pack",
    )(*(pltpu.with_memory_space_constraint(x, pltpu.HBM) for x in (key, value, grad, query, filters)))


def unpack(received, key, value, grad, filters):
    shape = jax.ShapeDtypeStruct(key.shape, BF16)
    rows = key.shape[1] // CH
    return pl.pallas_call(
        unpack_kernel,
        out_shape=(shape, shape, shape, jax.ShapeDtypeStruct(filters.shape, F32)),
        scratch_shapes=[pltpu.VMEM((2, rows, 128), F32), pltpu.VMEM((NZ * ZBACK, 128), F32)],
        compiler_params=params(8),
        name="unpack",
    )(received, key, value, grad)


def inward(received):
    return pl.pallas_call(
        inward_kernel,
        out_shape=jax.ShapeDtypeStruct((NPLANE * PROWS, 128), BF16),
        scratch_shapes=[pltpu.VMEM((NZ * ZROWS, 128), F32), pltpu.VMEM((NPLANE * PROWS, 128), F32)],
        compiler_params=params(8),
        name="inward",
    )(received)


def outward(received):
    return pl.pallas_call(
        outward_kernel,
        out_shape=jax.ShapeDtypeStruct((NZ * ZBACK, 128), BF16),
        scratch_shapes=[pltpu.VMEM((NPLANE * PBACK, 128), F32), pltpu.VMEM((NZ * ZBACK, 128), F32)],
        compiler_params=params(8),
        name="outward",
    )(received)


def group(received):
    count = NZ * NPLANE
    return pl.pallas_call(
        group_kernel,
        out_shape=jax.ShapeDtypeStruct((NPLANE * PBACK, 128), BF16),
        scratch_shapes=[
            pltpu.VMEM(received.shape, F32),
            pltpu.VMEM((2, count, 128), F32),
            pltpu.VMEM((count, TOK * ROWS), BF16),
            pltpu.VMEM((count, TOK * count), BF16),
            pltpu.VMEM((TOK * ROWS, count), BF16),
            pltpu.VMEM((TOK * ROWS, count), BF16),
            pltpu.VMEM((2 * ROWS, TOK * count), BF16),
        ],
        compiler_params=params(32),
        name="group",
    )(received)


def exchange(rows, axes, unit=4):
    chunks = rows.reshape(-1, unit, 128)
    return lax.all_to_all(chunks, axes, 0, 0, tiled=True).reshape(rows.shape)


def on_device(query_gate, key_gate, value_proj, grad_out, long_filters):
    rows = pack(query_gate, key_gate, value_proj, grad_out, long_filters)
    rows = inward(exchange(rows, Z_AXES))
    rows = group(exchange(rows, PLANE_AXES))
    rows = outward(exchange(rows, PLANE_AXES))
    return unpack(exchange(rows, Z_AXES, 2), key_gate, value_proj, grad_out, long_filters)


def solution(mesh):
    fine = Mesh(mesh.devices.reshape(NX, NZH, NCORE, NZL, NY), ("x", "zh", "core", "zl", "y"))
    tokens = P(("x", "zh", "core", "zl", "y"), None)
    filters = P(("zl", "y"), ("x", "zh", "core"))
    return jax.shard_map(
        on_device,
        mesh=fine,
        in_specs=(tokens, tokens, tokens, tokens, filters),
        out_specs=(tokens, tokens, tokens, filters),
        check_vma=False,
    )
```
